32 devices in a mesh: dp: 4 (over y, x), pipe: 2 (over core), tensor: 4 (over z).
Axes of the slice: x: 2, y: 2, z: 4, core: 2. Of those that a mesh axis runs over, the one named last changes fastest.
Arguments:
- stream_in: bfloat16 [768, 1536], P('dp'), may hold values from -6 to 6
- segment_ids: int32 [4, 192], P('dp'), may hold values from 0 to 7, never falling along the last dimension, each value on 1 to 96 neighbouring positions
- master_q: float32 [2, 1536, 1536], P('pipe', 'dp', 'tensor')
- moment_q: float32 [2, 1536, 1536], P('pipe', 'dp', 'tensor'), may hold values from -0.046875 to 0.046875
- second_q: float32 [2, 1536, 1536], P('pipe', 'dp', 'tensor'), may hold values from 1e-08 to 1e-06
- grad_q: float32 [2, 1536, 1536], P('pipe', 'dp', 'tensor'), may hold values from -0.15625 to 0.15625
- master_kv: float32 [2, 1536, 512], P('pipe', 'dp', 'tensor')
- moment_kv: float32 [2, 1536, 512], P('pipe', 'dp', 'tensor'), may hold values from -0.046875 to 0.046875
- second_kv: float32 [2, 1536, 512], P('pipe', 'dp', 'tensor'), may hold values from 1e-08 to 1e-06
- grad_kv: float32 [2, 1536, 512], P('pipe', 'dp', 'tensor'), may hold values from -0.15625 to 0.15625
Outputs:
- new_master_q: float32 [2, 1536, 1536], P('pipe', 'dp', 'tensor')
- new_moment_q: float32 [2, 1536, 1536], P('pipe', 'dp', 'tensor')
- new_second_q: float32 [2, 1536, 1536], P('pipe', 'dp', 'tensor')
- new_master_kv: float32 [2, 1536, 512], P('pipe', 'dp', 'tensor')
- new_moment_kv: float32 [2, 1536, 512], P('pipe', 'dp', 'tensor')
- new_second_kv: float32 [2, 1536, 512], P('pipe', 'dp', 'tensor')
- streams_out: bfloat16 [2, 768, 1536], P('pipe', 'dp', 'tensor')
The draws below stay inside these ranges and needn't reach their ends.
Inputs may be any that keep to these rules, and one draw needn't show every extreme that they name: `segment_ids`: in each row, document numbers never fall and start at 0; every document holds 1 to 96 tokens, one exactly 96.
All inputs are finite; a program needn't handle non-finite values.
Results may differ from the reference program's by a relative error of at most 0.0075.
The reference program's roundings to bfloat16 on the way count: a program that leaves them out, or rounds other values in their place, can miss the bound.
Values may be sent and summed in bfloat16 or wider, within the bound.
A program may use at most 64 MiB of HBM per device.

```python
import math
import jax
import jax.numpy as jnp
import numpy as np
from jax import lax

HEAD_DIM = 128
HEADS_DEV = 3
DOCS = 8
TOK = 192
HEADS = 12
KV_HEADS = 2
D = 1536
KV_COLS = 512
N_DP = 4
N_PIPE = 2


def projection_draw(key, shape_out, fan_in):
    return jax.random.normal(jax.random.fold_in(key, 5), shape_out, jnp.float32) * fan_in ** (-0.5)


def draw_master_q(key, part):
    return projection_draw(jax.random.fold_in(key, 101), (N_PIPE, D, HEADS * HEAD_DIM), D).astype(jnp.float32)


def draw_master_kv(key, part):
    return projection_draw(jax.random.fold_in(key, 202), (N_PIPE, D, KV_COLS), D).astype(jnp.float32)


def steps_of(stream_key, extent, cuts, smallest, top_value):
    gain, own = 1.0, jax.random.fold_in(stream_key, 6)
    for dim, parts in cuts:
        heights = jnp.exp(jax.random.uniform(jax.random.fold_in(own, dim), (parts,), jnp.float32, smallest / len(cuts), top_value / len(cuts)))
        gain = gain * jnp.repeat(heights, extent[dim] // parts).reshape([-1 if axis == dim else 1 for axis in range(len(extent))])
    return gain


def split_up(count, total, bound, skew):
    weights = [(1 << 20) // math.isqrt(rank ** skew) + 1 for rank in range(2, count + 1)]
    spare, counts = total - bound - (count - 1), [1] * (count - 1)
    while spare > 0:
        movable = [i for i in range(count - 1) if counts[i] < bound]
        whole, remaining = sum([weights[i] for i in movable]), spare
        for i in movable:
            extra = min(bound - counts[i], max(1, remaining * weights[i] // whole), spare)
            counts[i] = counts[i] + extra
            spare = spare - extra
    return np.array([bound] + counts)


def uneven_parts(stream_key, number_of, total, most, lean):
    if number_of == 2:
        one = jax.random.randint(stream_key, (), max(1, total - most), min(most, total - 1) + 1)
        return jnp.stack([one, total - one])
    sizes = jnp.asarray(split_up(number_of, total, most, lean), jnp.int32)
    couples = (number_of - 1) // 2
    source_of, receiver = sizes[1:1 + 2 * couples:2], sizes[2:2 + 2 * couples:2]
    slack = jnp.minimum(source_of - 1, most - receiver)
    shifted = jax.random.randint(jax.random.fold_in(stream_key, 1), (couples,), 0, 1 << 20) % (slack + 1)
    sizes = sizes.at[1:1 + 2 * couples:2].set(source_of - shifted).at[2:2 + 2 * couples:2].set(receiver + shifted)
    return sizes[jax.random.permutation(jax.random.fold_in(stream_key, 2), number_of)]


def bell_draw(key, dims, deviation, bound, split=(), held_as=jnp.bfloat16):
    values = jax.random.normal(key, dims, jnp.float32) * deviation
    if len(split) > 0:
        values = steps_of(key, dims, split, -0.22, 0.18) * values
    return jnp.clip(values, min=-bound, max=bound).astype(held_as)


def setup_inputs(seed: int = 0) -> dict:
    streams_of = jax.random.split(jax.random.key(seed), 11)
    return {
        "stream_in": bell_draw(streams_of[0], (N_DP * TOK, D), 1.0, 6.0, ((0, 4),)),
        "segment_ids": jax.vmap(lambda own: jnp.searchsorted(jnp.cumsum(uneven_parts(own, DOCS, TOK, TOK // 2, 2)), jnp.arange(TOK), side="right"))(jax.random.split(streams_of[1], N_DP)).reshape((N_DP, TOK)).astype(jnp.int32),
        "master_q": draw_master_q(jax.random.fold_in(streams_of[10], 71), 0),
        "moment_q": bell_draw(streams_of[3], (N_PIPE, D, HEADS * HEAD_DIM), 0.003, 0.046875, ((0, 2), (1, 4), (2, 4)), jnp.float32),
        "second_q": jnp.clip(jnp.exp(math.log(9.999999974752427e-07) - 4.6051702 * jax.random.uniform(streams_of[4], (N_PIPE, D, HEADS * HEAD_DIM), jnp.float32) ** steps_of(streams_of[4], (N_PIPE, D, HEADS * HEAD_DIM), ((0, 2), (1, 4), (2, 4)), -0.2, 0.2)), 9.99999993922529e-09, 9.999999974752427e-07),
        "grad_q": bell_draw(streams_of[5], (N_PIPE, D, HEADS * HEAD_DIM), 0.01, 0.15625, ((0, 2), (1, 4), (2, 4)), jnp.float32),
        "master_kv": draw_master_kv(jax.random.fold_in(streams_of[10], 71), 0),
        "moment_kv": bell_draw(streams_of[7], (N_PIPE, D, KV_COLS), 0.003, 0.046875, ((0, 2), (1, 4), (2, 4)), jnp.float32),
        "second_kv": jnp.clip(jnp.exp(math.log(9.999999974752427e-07) - 4.6051702 * jax.random.uniform(streams_of[8], (N_PIPE, D, KV_COLS), jnp.float32) ** steps_of(streams_of[8], (N_PIPE, D, KV_COLS), ((0, 2), (1, 4), (2, 4)), -0.2, 0.2)), 9.99999993922529e-09, 9.999999974752427e-07),
        "grad_kv": bell_draw(streams_of[9], (N_PIPE, D, KV_COLS), 0.01, 0.15625, ((0, 2), (1, 4), (2, 4)), jnp.float32),
    }


beta_one = 0.9
beta_two = 0.999
adam_eps = 1e-08
learn_rate = 0.003
decay_rate = 0.1
adam_step = 10.0
norm_eps = 1e-05

def adamw(master, moment, second, gradient):
    moment_new = beta_one * moment + (1.0 - beta_one) * gradient
    second_new = beta_two * second + (1.0 - beta_two) * gradient * gradient
    fix_one = 1.0 - beta_one ** adam_step
    fix_two = 1.0 - beta_two ** adam_step
    step_dir = moment_new / fix_one / (jnp.sqrt(second_new / fix_two) + adam_eps)
    master_new = master - learn_rate * (step_dir + decay_rate * master)
    return (master_new, moment_new, second_new)

def doc_positions(segments):
    length = segments.shape[0]
    same_doc = segments[:, None] == segments[None, :]
    rows_idx = jnp.arange(length, dtype=jnp.int32)
    earlier = rows_idx[None, :] < rows_idx[:, None]
    positions = lax.optimization_barrier(jnp.sum(jnp.where(same_doc & earlier, 1, 0).astype(jnp.int32), axis=1))
    allowed = same_doc & (rows_idx[None, :] <= rows_idx[:, None])
    return (positions, allowed)

def rotation_tables(positions):
    half_dim = HEAD_DIM // 2
    inverse_freq = 10000.0 ** (-2.0 * jnp.arange(half_dim, dtype=jnp.float32) / HEAD_DIM)
    angles = positions.astype(jnp.float32)[:, None] * inverse_freq[None, :]
    cosine = jnp.concatenate([jnp.cos(angles), jnp.cos(angles)], axis=1)
    sine_tab = jnp.concatenate([jnp.sin(angles), jnp.sin(angles)], axis=1)
    return (cosine, sine_tab)

def rotate(values, cosine, sine_tab):
    half_dim = HEAD_DIM // 2
    turned = jnp.concatenate([-values[..., half_dim:], values[..., :half_dim]], axis=-1)
    return values * cosine[:, None, :] + turned * sine_tab[:, None, :]

def norm_rows(stream):
    widened = stream.astype(jnp.float32)
    scale_rows = lax.rsqrt(lax.optimization_barrier(jnp.mean(widened * widened, axis=1, keepdims=True)) + norm_eps)
    return (widened * scale_rows).astype(jnp.bfloat16)

def spread_heads(per_kv):
    repeated = jnp.repeat(per_kv, HEADS_DEV, axis=1)
    return jnp.tile(repeated, (1, HEADS // (HEADS_DEV * KV_HEADS), 1))

def section(stream, allowed, cosine, sine_tab, weight_q, weight_kv):
    length = stream.shape[0]
    normed = norm_rows(stream)
    queries = jnp.dot(normed, weight_q, preferred_element_type=jnp.float32).reshape(length, HEADS, HEAD_DIM)
    paired = jnp.dot(normed, weight_kv, preferred_element_type=jnp.float32).reshape(length, 2, KV_HEADS, HEAD_DIM)
    queries = rotate(queries, cosine, sine_tab).astype(jnp.bfloat16)
    keys_bf = rotate(paired[:, 0], cosine, sine_tab).astype(jnp.bfloat16)
    values_bf = paired[:, 1].astype(jnp.bfloat16)
    keys_all = spread_heads(keys_bf)
    values_all = spread_heads(values_bf)
    scores = jnp.einsum('qhd,khd->hqk', queries.astype(jnp.float32), keys_all.astype(jnp.float32)) * HEAD_DIM ** (-0.5)
    scores = jnp.where(allowed[None], scores, -1e+30)
    row_max = lax.optimization_barrier(jnp.max(scores, axis=2, keepdims=True))
    exp_terms = jnp.exp(scores - row_max)
    weights_bf = (exp_terms / lax.optimization_barrier(jnp.sum(exp_terms, axis=2, keepdims=True))).astype(jnp.bfloat16)
    mixed = jnp.einsum('hqk,khd->qhd', weights_bf.astype(jnp.float32), values_all.astype(jnp.float32))
    mixed = mixed.reshape(length, HEADS * HEAD_DIM)
    return (stream.astype(jnp.float32) + mixed).astype(jnp.bfloat16)

def reference(stream_in, segment_ids, master_q, moment_q, second_q, grad_q, master_kv, moment_kv, second_kv, grad_kv):
    new_q = adamw(master_q, moment_q, second_q, grad_q)
    new_kv = adamw(master_kv, moment_kv, second_kv, grad_kv)
    weight_q = new_q[0].astype(jnp.bfloat16)
    weight_kv = new_kv[0].astype(jnp.bfloat16)
    streams = stream_in.reshape(N_DP, TOK, D)

    def replica(packed):
        stream, segments = packed
        positions, allowed = doc_positions(segments)
        cosine, sine_tab = rotation_tables(positions)
        first_out = section(stream, allowed, cosine, sine_tab, weight_q[0], weight_kv[0])
        second_out = section(first_out, allowed, cosine, sine_tab, weight_q[1], weight_kv[1])
        return jnp.stack([first_out, second_out])
    outputs = lax.map(replica, (streams, segment_ids))
    result = jnp.transpose(outputs, (1, 0, 2, 3)).reshape(N_PIPE, N_DP * TOK, D)
    return (new_q[0], new_q[1], new_q[2], new_kv[0], new_kv[1], new_kv[2], result)
```

```python
import functools

import jax
import jax.numpy as jnp
from jax import lax
from jax.experimental import pallas as pl
from jax.experimental.pallas import tpu as pltpu
from jax.sharding import PartitionSpec as P

HEAD_DIM = 128
MESH = pl.DeviceIdType.MESH

beta_one = 0.9
beta_two = 0.999
adam_eps = 1e-08
learn_rate = 0.003
decay_rate = 0.1
adam_step = 10.0
norm_eps = 1e-05


def adamw(master, moment, second, gradient):
    moment_new = beta_one * moment + (1.0 - beta_one) * gradient
    second_new = beta_two * second + (1.0 - beta_two) * gradient * gradient
    fix_one = 1.0 - beta_one**adam_step
    fix_two = 1.0 - beta_two**adam_step
    step_dir = moment_new / fix_one / (jnp.sqrt(second_new / fix_two) + adam_eps)
    master_new = master - learn_rate * (step_dir + decay_rate * master)
    return (master_new, moment_new, second_new)


def write_kernel(*refs):
    count = (len(refs) - 1) // 2
    sems = refs[-1]
    copies = [
        pltpu.make_async_copy(refs[i], refs[count + i], sems.at[i]) for i in range(count)
    ]
    for copy in copies:
        copy.start()
    for copy in copies:
        copy.wait()


def write_call(arrays):
    return pl.pallas_call(
        write_kernel,
        in_specs=[pl.BlockSpec(memory_space=pltpu.VMEM)] * len(arrays),
        out_specs=[pl.BlockSpec(memory_space=pl.ANY)] * len(arrays),
        out_shape=[jax.ShapeDtypeStruct(a.shape, a.dtype) for a in arrays],
        scratch_shapes=[pltpu.SemaphoreType.DMA((len(arrays),))],
    )(*[pltpu.with_memory_space_constraint(a, pltpu.VMEM) for a in arrays])


def sections_kernel(
    n_dp,
    n_tensor,
    x_hbm,
    seg_hbm,
    mq_hbm,
    eq_hbm,
    sq_hbm,
    gq_hbm,
    mk_hbm,
    ek_hbm,
    sk_hbm,
    gk_hbm,
    nmq,
    neq,
    nsq,
    nmk,
    nek,
    nsk,
    out_ref,
    x_ref,
    seg_ref,
    q_ref,
    k_ref,
    load_sem,
    gathered,
    normed_ref,
    cos_ref,
    sin_ref,
    mask_ref,
    kv_ref,
    queries_ref,
    first_ref,
    stream_ref,
    send_sem,
    recv_sem,
    pair_sem,
    stream_send,
    stream_recv,
    go_sem,
):
    dp = lax.axis_index("dp")
    pipe = lax.axis_index("pipe")
    tensor = lax.axis_index("tensor")
    tokens, features = x_ref.shape
    rows = q_ref.shape[1]
    heads = first_ref.shape[0]
    n_pieces = 1 + heads
    half = n_tensor // 2
    half_rows = rows // 2
    relayed = n_dp == 4
    holds_key = tensor < half
    pair = lax.rem(tensor + half, n_tensor)
    slot = jnp.where(holds_key, 0, 1)
    f32 = jnp.float32
    bf16 = jnp.bfloat16

    x_side = dp + 1 - 2 * lax.rem(dp, 2)
    y_side = lax.rem(dp + 2, 4)

    load_x = pltpu.make_async_copy(x_hbm, x_ref, load_sem.at[8])
    load_seg = pltpu.make_async_copy(seg_hbm, seg_ref, load_sem.at[9])
    loads_k = [
        pltpu.make_async_copy(ref.at[0], k_ref.at[i], load_sem.at[i])
        for i, ref in enumerate((mk_hbm, ek_hbm, sk_hbm, gk_hbm))
    ]
    loads_q = [
        pltpu.make_async_copy(ref.at[0], q_ref.at[i], load_sem.at[4 + i])
        for i, ref in enumerate((mq_hbm, eq_hbm, sq_hbm, gq_hbm))
    ]
    for load in loads_k + loads_q + [load_x, load_seg]:
        load.start()

    barrier = pltpu.get_barrier_semaphore()
    if relayed:
        near = [x_side, y_side]
    else:
        near = [lax.rem(dp + off, n_dp) for off in range(1, n_dp)]
    for peer in near:
        pl.semaphore_signal(
            barrier, inc=1, device_id=(peer, pipe, tensor), device_id_type=MESH
        )
    pl.semaphore_signal(barrier, inc=1, device_id=(dp, pipe, pair), device_id_type=MESH)
    for off in range(n_tensor):
        pl.semaphore_signal(
            barrier,
            inc=1,
            device_id=(dp, 1 - pipe, lax.rem(tensor + off, n_tensor)),
            device_id_type=MESH,
        )

    def norm(read_block):
        blocks = features // HEAD_DIM
        squares = jnp.zeros((tokens, HEAD_DIM), f32)
        for b in range(blocks):
            value = read_block(b)
            squares += value * value
        mean = jnp.sum(squares, axis=1, keepdims=True) / features
        scale = lax.rsqrt(mean + norm_eps)
        for b in range(blocks):
            normed_ref[:, b * HEAD_DIM : (b + 1) * HEAD_DIM] = (
                read_block(b) * scale
            ).astype(bf16)

    def tables():
        row = lax.broadcasted_iota(jnp.int32, (tokens, tokens), 0)
        col = lax.broadcasted_iota(jnp.int32, (tokens, tokens), 1)
        seg_row = jnp.broadcast_to(seg_ref[...].astype(f32), (tokens, tokens))
        seg_col = jnp.sum(jnp.where(row == col, seg_row, 0.0), axis=1, keepdims=True)
        same = seg_row == seg_col
        mask_ref[...] = jnp.where(same & (col <= row), 1.0, 0.0)
        position = jnp.sum(jnp.where(same & (col < row), 1.0, 0.0), axis=1, keepdims=True)
        lane = lax.broadcasted_iota(jnp.int32, (1, HEAD_DIM), 1)
        half_dim = HEAD_DIM // 2
        index = jnp.where(lane < half_dim, lane, lane - half_dim).astype(f32)
        inverse_freq = 10000.0 ** (-2.0 * index / HEAD_DIM)
        angles = position * inverse_freq
        cos_ref[...] = jnp.cos(angles)
        sine = jnp.sin(angles)
        sin_ref[...] = jnp.where(lane < half_dim, -sine, sine)

    step_rows = 48 if rows % 48 == 0 else rows

    def update_k(i, carry):
        at = pl.ds(pl.multiple_of(i * step_rows, step_rows), step_rows)
        new = adamw(k_ref[0, at], k_ref[1, at], k_ref[2, at], k_ref[3, at])
        nmk[0, at], nek[0, at], nsk[0, at] = new
        gathered[0, dp, at] = new[0].astype(bf16)
        return carry

    def update_q(head):
        columns = slice(head * HEAD_DIM, (head + 1) * HEAD_DIM)

        def step(i, carry):
            at = pl.ds(pl.multiple_of(i * step_rows, step_rows), step_rows)
            new = adamw(*[q_ref[n, at, columns] for n in range(4)])
            nmq[0, at, columns], neq[0, at, columns], nsq[0, at, columns] = new
            gathered[1 + head, dp, at] = new[0].astype(bf16)
            return carry

        lax.fori_loop(0, rows // step_rows, step, 0)

    part_a = pl.ds(0, half_rows)
    part_b = pl.ds(half_rows, half_rows)

    def copy_to(peer, ref, piece, kind):
        return pltpu.make_async_remote_copy(
            src_ref=ref,
            dst_ref=ref,
            send_sem=send_sem.at[piece, kind],
            recv_sem=recv_sem.at[piece, kind],
            device_id=(peer, pipe, tensor),
            device_id_type=MESH,
        )

    def first_copies(piece):
        if relayed:
            return [
                copy_to(x_side, gathered.at[piece, dp, part_a], piece, 0),
                copy_to(y_side, gathered.at[piece, dp, part_b], piece, 1),
            ]
        return [
            copy_to(lax.rem(dp + off, n_dp), gathered.at[piece, dp], piece, off - 1)
            for off in range(1, n_dp)
        ]

    def second_copies(piece):
        if not relayed:
            return []
        return [
            copy_to(x_side, gathered.at[piece, dp, part_b], piece, 2),
            copy_to(y_side, gathered.at[piece, dp, part_a], piece, 3),
        ]

    def relay_copies(piece):
        if not relayed:
            return []
        return [
            copy_to(y_side, gathered.at[piece, x_side, part_a], piece, 4),
            copy_to(x_side, gathered.at[piece, y_side, part_b], piece, 5),
        ]

    def start(copies):
        for copy in copies:
            copy.start()

    def relay(piece):
        if not relayed:
            return
        for got, passed in zip(first_copies(piece), relay_copies(piece)):
            got.wait_recv()
            passed.start()

    def arrived(piece):
        copies = second_copies(piece) + relay_copies(piece)
        for copy in copies if relayed else first_copies(piece):
            copy.wait_recv()

    def all_sent(piece):
        for copy in first_copies(piece) + second_copies(piece) + relay_copies(piece):
            copy.wait_send()

    def weights(piece):
        return gathered[piece].reshape(n_dp * rows, HEAD_DIM)

    def rope(values, cosine, sine):
        return values * cosine + pltpu.roll(values, HEAD_DIM // 2, 1) * sine

    def key_or_value(values, is_key):
        cosine = jnp.where(is_key, cos_ref[...], 1.0)
        sine = jnp.where(is_key, sin_ref[...], 0.0)
        return rope(values, cosine, sine).astype(bf16)

    def project(head):
        queries = jnp.dot(normed_ref[...], weights(1 + head), preferred_element_type=f32)
        queries_ref[head] = rope(queries, cos_ref[...], sin_ref[...]).astype(bf16)

    def attend(head, residual):
        scores = lax.dot_general(
            queries_ref[head],
            kv_ref[0],
            (((1,), (1,)), ((), ())),
            preferred_element_type=f32,
        ) * HEAD_DIM ** (-0.5)
        scores = jnp.where(mask_ref[...] > 0.5, scores, -1e30)
        row_max = jnp.max(scores, axis=1, keepdims=True)
        terms = jnp.exp(scores - row_max)
        probs = (terms / jnp.sum(terms, axis=1, keepdims=True)).astype(bf16)
        mixed = jnp.dot(probs, kv_ref[1], preferred_element_type=f32)
        return (residual.astype(f32) + mixed).astype(bf16)

    def pair_block(source, target):
        return pltpu.make_async_remote_copy(
            src_ref=source,
            dst_ref=target,
            send_sem=pair_sem.at[0],
            recv_sem=pair_sem.at[1],
            device_id=(dp, pipe, pair),
            device_id_type=MESH,
        )

    def stream_copy(head, to_tensor):
        return pltpu.make_async_remote_copy(
            src_ref=first_ref.at[head],
            dst_ref=stream_ref.at[tensor * heads + head],
            send_sem=stream_send.at[head, to_tensor],
            recv_sem=stream_recv.at[tensor * heads + head],
            device_id=(dp, 1, to_tensor),
            device_id_type=MESH,
        )

    weight_exchange = pair_block(gathered.at[0, dp], gathered.at[n_pieces, dp])

    for load in loads_k:
        load.wait()
    lax.fori_loop(0, rows // step_rows, update_k, 0)
    pl.semaphore_wait(barrier, len(near) + 1 + n_tensor)

    @pl.when(pipe == 0)
    def _():
        start(first_copies(0) + second_copies(0))

    @pl.when(pipe == 1)
    def _():
        weight_exchange.start()

    for load in loads_q:
        load.wait()
    update_q(0)

    @pl.when(pipe == 0)
    def _():
        start(first_copies(1))

    for head in range(1, heads):
        update_q(head)
    load_x.wait()
    load_seg.wait()

    @pl.when(pipe == 0)
    def _():
        norm(lambda b: x_ref[:, b * HEAD_DIM : (b + 1) * HEAD_DIM].astype(f32))
        tables()
        exchange = pair_block(kv_ref.at[slot], kv_ref.at[slot])
        for p in range(n_pieces):
            relay(p)
            if p + 1 < n_pieces:
                start(second_copies(p + 1))
            if p + 2 < n_pieces:
                start(first_copies(p + 2))
            if p == 1:
                arrived(0)
                block = jnp.dot(normed_ref[...], weights(0), preferred_element_type=f32)
                kv_ref[slot] = key_or_value(block, holds_key)
                exchange.start()
            if p == 2:
                arrived(1)
                project(0)
        pl.semaphore_signal(
            go_sem, inc=1, device_id=(dp, 1, tensor), device_id_type=MESH
        )
        for head in range(1, heads):
            arrived(1 + head)
            project(head)
        exchange.wait()
        for head in range(heads):
            columns = pl.ds(
                pl.multiple_of((tensor * heads + head) * HEAD_DIM, HEAD_DIM), HEAD_DIM
            )
            result = attend(head, x_ref[:, columns])
            first_ref[head] = result
            for t in range(n_tensor):
                stream_copy(head, t).start()
            out_ref[:, head * HEAD_DIM : (head + 1) * HEAD_DIM] = result
        for p in range(n_pieces):
            all_sent(p)
        for head in range(heads):
            for t in range(n_tensor):
                stream_copy(head, t).wait_send()

    @pl.when(pipe == 1)
    def _():
        tables()
        weight_exchange.wait()
        order = [0, n_pieces] + list(range(1, n_pieces))
        pl.semaphore_wait(go_sem, 1)
        start(first_copies(order[0]) + second_copies(order[0]) + first_copies(order[1]))
        for i, p in enumerate(order):
            relay(p)
            if i + 1 < len(order):
                start(second_copies(order[i + 1]))
            if i + 2 < len(order):
                start(first_copies(order[i + 2]))

        for t in range(n_tensor):
            for head in range(heads):
                pltpu.make_async_remote_copy(
                    src_ref=first_ref.at[head],
                    dst_ref=stream_ref.at[t * heads + head],
                    send_sem=stream_send.at[head, t],
                    recv_sem=stream_recv.at[t * heads + head],
                    device_id=(dp, 0, tensor),
                    device_id_type=MESH,
                ).wait_recv()
        norm(lambda b: stream_ref[b].astype(f32))
        for p in order:
            arrived(p)
        block = jnp.dot(normed_ref[...], weights(0), preferred_element_type=f32)
        kv_ref[slot] = key_or_value(block, holds_key)
        block = jnp.dot(normed_ref[...], weights(n_pieces), preferred_element_type=f32)
        kv_ref[1 - slot] = key_or_value(block, jnp.logical_not(holds_key))
        for head in range(heads):
            project(head)
        for head in range(heads):
            out_ref[:, head * HEAD_DIM : (head + 1) * HEAD_DIM] = attend(
                head, stream_ref[tensor * heads + head]
            )
        for p in order:
            all_sent(p)


def sections_call(n_dp, n_tensor, stream, segments, q_arrays, kv_arrays):
    tokens, features = stream.shape
    _, rows, q_cols = q_arrays[0].shape
    kv_cols = kv_arrays[0].shape[2]
    heads = q_cols // HEAD_DIM
    n_pieces = 1 + heads
    kinds = 6 if n_dp == 4 else n_dp - 1
    bf16 = jnp.bfloat16
    f32 = jnp.float32
    vmem = pl.BlockSpec(memory_space=pltpu.VMEM)
    anywhere = pl.BlockSpec(memory_space=pl.ANY)
    return pl.pallas_call(
        functools.partial(sections_kernel, n_dp, n_tensor),
        out_shape=[pltpu.VMEM((1, rows, q_cols), f32)] * 3
        + [pltpu.VMEM((1, rows, kv_cols), f32)] * 3
        + [pltpu.VMEM((tokens, q_cols), bf16)],
        in_specs=[anywhere] * 10,
        out_specs=[vmem] * 7,
        scratch_shapes=[
            pltpu.VMEM((tokens, features), bf16),
            pltpu.VMEM(segments.shape, jnp.int32),
            pltpu.VMEM((4, rows, q_cols), f32),
            pltpu.VMEM((4, rows, kv_cols), f32),
            pltpu.SemaphoreType.DMA((10,)),
            pltpu.VMEM((n_pieces + 1, n_dp, rows, HEAD_DIM), bf16),
            pltpu.VMEM((tokens, features), bf16),
            pltpu.VMEM((tokens, HEAD_DIM), jnp.float32),
            pltpu.VMEM((tokens, HEAD_DIM), jnp.float32),
            pltpu.VMEM((tokens, tokens), jnp.float32),
            pltpu.VMEM((2, tokens, HEAD_DIM), bf16),
            pltpu.VMEM((heads, tokens, HEAD_DIM), bf16),
            pltpu.VMEM((heads, tokens, HEAD_DIM), bf16),
            pltpu.VMEM((n_tensor * heads, tokens, HEAD_DIM), bf16),
            pltpu.SemaphoreType.DMA((n_pieces + 1, kinds)),
            pltpu.SemaphoreType.DMA((n_pieces + 1, kinds)),
            pltpu.SemaphoreType.DMA((2,)),
            pltpu.SemaphoreType.DMA((heads, n_tensor)),
            pltpu.SemaphoreType.DMA((n_tensor * heads,)),
            pltpu.SemaphoreType.REGULAR,
        ],
        compiler_params=pltpu.CompilerParams(collective_id=0, has_side_effects=True),
    )(stream, segments, *q_arrays, *kv_arrays)


def solution(mesh):
    n_dp, n_tensor = mesh.shape["dp"], mesh.shape["tensor"]

    def on_device(
        stream_in,
        segment_ids,
        master_q,
        moment_q,
        second_q,
        grad_q,
        master_kv,
        moment_kv,
        second_kv,
        grad_kv,
    ):
        fresh = sections_call(
            n_dp,
            n_tensor,
            stream_in,
            segment_ids,
            (master_q, moment_q, second_q, grad_q),
            (master_kv, moment_kv, second_kv, grad_kv),
        )
        *states, result = write_call(fresh)
        return (*states, result[None])

    weight_spec = P("pipe", "dp", "tensor")
    return jax.shard_map(
        on_device,
        mesh=mesh,
        in_specs=(P("dp", None), P("dp", None)) + (weight_spec,) * 8,
        out_specs=(weight_spec,) * 7,
        check_vma=False,
    )
```

```python
import functools

import jax
import jax.numpy as jnp
from jax import lax
from jax.experimental import pallas as pl
from jax.experimental.pallas import tpu as pltpu
from jax.sharding import PartitionSpec as P

HEAD_DIM = 128
MESH = pl.DeviceIdType.MESH

beta_one = 0.9
beta_two = 0.999
adam_eps = 1e-08
learn_rate = 0.003
decay_rate = 0.1
adam_step = 10.0
norm_eps = 1e-05


def adamw(master, moment, second, gradient):
    moment_new = beta_one * moment + (1.0 - beta_one) * gradient
    second_new = beta_two * second + (1.0 - beta_two) * gradient * gradient
    fix_one = 1.0 - beta_one**adam_step
    fix_two = 1.0 - beta_two**adam_step
    step_dir = moment_new / fix_one / (jnp.sqrt(second_new / fix_two) + adam_eps)
    master_new = master - learn_rate * (step_dir + decay_rate * master)
    return (master_new, moment_new, second_new)


def write_kernel(*refs):
    count = (len(refs) - 1) // 2
    sems = refs[-1]
    copies = [
        pltpu.make_async_copy(refs[i], refs[count + i], sems.at[i]) for i in range(count)
    ]
    for copy in copies:
        copy.start()
    for copy in copies:
        copy.wait()


def write_call(arrays):
    return pl.pallas_call(
        write_kernel,
        in_specs=[pl.BlockSpec(memory_space=pltpu.VMEM)] * len(arrays),
        out_specs=[pl.BlockSpec(memory_space=pl.ANY)] * len(arrays),
        out_shape=[jax.ShapeDtypeStruct(a.shape, a.dtype) for a in arrays],
        scratch_shapes=[pltpu.SemaphoreType.DMA((len(arrays),))],
    )(*[pltpu.with_memory_space_constraint(a, pltpu.VMEM) for a in arrays])


def sections_kernel(
    n_dp,
    n_tensor,
    x_hbm,
    seg_hbm,
    mq_hbm,
    eq_hbm,
    sq_hbm,
    gq_hbm,
    mk_hbm,
    ek_hbm,
    sk_hbm,
    gk_hbm,
    nmq,
    neq,
    nsq,
    nmk,
    nek,
    nsk,
    out_ref,
    x_ref,
    seg_ref,
    q_ref,
    k_ref,
    load_sem,
    gathered,
    normed_ref,
    cos_ref,
    sin_ref,
    mask_ref,
    kv_ref,
    queries_ref,
    sums_ref,
    first_ref,
    stream_ref,
    send_sem,
    recv_sem,
    pair_sem,
    stream_send,
    stream_recv,
    go_sem,
):
    dp = lax.axis_index("dp")
    pipe = lax.axis_index("pipe")
    tensor = lax.axis_index("tensor")
    tokens, features = x_ref.shape
    rows = q_ref.shape[1]
    heads = first_ref.shape[0]
    n_pieces = 1 + heads
    half = n_tensor // 2
    half_rows = rows // 2
    relayed = n_dp == 4
    holds_key = tensor < half
    pair = lax.rem(tensor + half, n_tensor)
    slot = jnp.where(holds_key, 0, 1)
    f32 = jnp.float32
    bf16 = jnp.bfloat16

    if n_tensor == 4:
        low = tensor < 2
        far_first = [
            jnp.where(low, 3, 0),
            jnp.where(low, 2, 1),
            tensor + 1 - 2 * lax.rem(tensor, 2),
            tensor,
        ]
    else:
        far_first = [lax.rem(tensor + off, n_tensor) for off in range(n_tensor)]
    blockwise = rows == heads * HEAD_DIM and n_dp == n_tensor

    x_side = dp + 1 - 2 * lax.rem(dp, 2)
    y_side = lax.rem(dp + 2, 4)

    load_x = pltpu.make_async_copy(x_hbm, x_ref, load_sem.at[8])
    load_seg = pltpu.make_async_copy(seg_hbm, seg_ref, load_sem.at[9])
    loads_k = [
        pltpu.make_async_copy(ref.at[0], k_ref.at[i], load_sem.at[i])
        for i, ref in enumerate((mk_hbm, ek_hbm, sk_hbm, gk_hbm))
    ]
    loads_q = [
        pltpu.make_async_copy(ref.at[0], q_ref.at[i], load_sem.at[4 + i])
        for i, ref in enumerate((mq_hbm, eq_hbm, sq_hbm, gq_hbm))
    ]
    for load in loads_k + loads_q + [load_x, load_seg]:
        load.start()

    barrier = pltpu.get_barrier_semaphore()
    if relayed:
        near = [x_side, y_side, 3 - dp]
    else:
        near = [lax.rem(dp + off, n_dp) for off in range(1, n_dp)]
    for peer in near:
        pl.semaphore_signal(
            barrier, inc=1, device_id=(peer, pipe, tensor), device_id_type=MESH
        )
    pl.semaphore_signal(barrier, inc=1, device_id=(dp, pipe, pair), device_id_type=MESH)
    for off in range(n_tensor):
        pl.semaphore_signal(
            barrier,
            inc=1,
            device_id=(dp, 1 - pipe, lax.rem(tensor + off, n_tensor)),
            device_id_type=MESH,
        )

    def norm(read_block):
        blocks = features // HEAD_DIM
        squares = jnp.zeros((tokens, HEAD_DIM), f32)
        for b in range(blocks):
            value = read_block(b)
            squares += value * value
        mean = jnp.sum(squares, axis=1, keepdims=True) / features
        scale = lax.rsqrt(mean + norm_eps)
        for b in range(blocks):
            normed_ref[:, b * HEAD_DIM : (b + 1) * HEAD_DIM] = (
                read_block(b) * scale
            ).astype(bf16)

    def tables():
        row = lax.broadcasted_iota(jnp.int32, (tokens, tokens), 0)
        col = lax.broadcasted_iota(jnp.int32, (tokens, tokens), 1)
        seg_row = jnp.broadcast_to(seg_ref[...].astype(f32), (tokens, tokens))
        seg_col = jnp.sum(jnp.where(row == col, seg_row, 0.0), axis=1, keepdims=True)
        same = seg_row == seg_col
        mask_ref[...] = jnp.where(same & (col <= row), 1.0, 0.0)
        position = jnp.sum(jnp.where(same & (col < row), 1.0, 0.0), axis=1, keepdims=True)
        lane = lax.broadcasted_iota(jnp.int32, (1, HEAD_DIM), 1)
        half_dim = HEAD_DIM // 2
        index = jnp.where(lane < half_dim, lane, lane - half_dim).astype(f32)
        inverse_freq = 10000.0 ** (-2.0 * index / HEAD_DIM)
        angles = position * inverse_freq
        cos_ref[...] = jnp.cos(angles)
        sine = jnp.sin(angles)
        sin_ref[...] = jnp.where(lane < half_dim, -sine, sine)

    step_rows = 48 if rows % 48 == 0 else rows

    def update_k(i, carry):
        at = pl.ds(pl.multiple_of(i * step_rows, step_rows), step_rows)
        new = adamw(k_ref[0, at], k_ref[1, at], k_ref[2, at], k_ref[3, at])
        nmk[0, at], nek[0, at], nsk[0, at] = new
        gathered[0, dp, at] = new[0].astype(bf16)
        return carry

    def update_q(head):
        columns = slice(head * HEAD_DIM, (head + 1) * HEAD_DIM)

        def step(i, carry):
            at = pl.ds(pl.multiple_of(i * step_rows, step_rows), step_rows)
            new = adamw(*[q_ref[n, at, columns] for n in range(4)])
            nmq[0, at, columns], neq[0, at, columns], nsq[0, at, columns] = new
            gathered[1 + head, dp, at] = new[0].astype(bf16)
            return carry

        lax.fori_loop(0, rows // step_rows, step, 0)

    part_a = pl.ds(0, half_rows)
    part_b = pl.ds(half_rows, half_rows)

    def copy_to(peer, ref, piece, kind):
        return pltpu.make_async_remote_copy(
            src_ref=ref,
            dst_ref=ref,
            send_sem=send_sem.at[piece, kind],
            recv_sem=recv_sem.at[piece, kind],
            device_id=(peer, pipe, tensor),
            device_id_type=MESH,
        )

    def direct_copies(piece):
        own = gathered.at[piece, dp]
        if relayed:
            return [
                copy_to(3 - dp, own, piece, 0),
                copy_to(x_side, own, piece, 1),
                copy_to(y_side, own, piece, 2),
            ]
        return [copy_to(peer, own, piece, n) for n, peer in enumerate(near)]

    def own_copies(piece, kinds=range(4)):
        peers = (x_side, y_side, x_side, y_side)
        parts = (part_a, part_b, part_b, part_a)
        return [
            copy_to(peers[n], gathered.at[piece, dp, parts[n]], piece, n) for n in kinds
        ]

    def relay_copies(piece):
        return [
            copy_to(y_side, gathered.at[piece, x_side, part_a], piece, 4),
            copy_to(x_side, gathered.at[piece, y_side, part_b], piece, 5),
        ]

    def start(copies):
        for copy in copies:
            copy.start()

    def send(piece, direct):
        start(direct_copies(piece) if direct or not relayed else own_copies(piece))

    def relay(piece):
        if not relayed:
            return
        for got, passed in zip(own_copies(piece, (0, 1)), relay_copies(piece)):
            got.wait_recv()
            passed.start()

    def arrived(piece, direct):
        if direct or not relayed:
            copies = direct_copies(piece)
        else:
            copies = own_copies(piece, (2, 3)) + relay_copies(piece)
        for copy in copies:
            copy.wait_recv()

    def all_sent(piece, direct):
        if direct or not relayed:
            copies = direct_copies(piece)
        else:
            copies = own_copies(piece) + relay_copies(piece)
        for copy in copies:
            copy.wait_send()

    def weights(piece):
        return gathered[piece].reshape(n_dp * rows, HEAD_DIM)

    def rope(values, cosine, sine):
        return values * cosine + pltpu.roll(values, HEAD_DIM // 2, 1) * sine

    def key_or_value(values, is_key):
        cosine = jnp.where(is_key, cos_ref[...], 1.0)
        sine = jnp.where(is_key, sin_ref[...], 0.0)
        return rope(values, cosine, sine).astype(bf16)

    def project(head):
        queries = jnp.dot(normed_ref[...], weights(1 + head), preferred_element_type=f32)
        queries_ref[head] = rope(queries, cos_ref[...], sin_ref[...]).astype(bf16)

    def mix(queries):
        scores = lax.dot_general(
            queries, kv_ref[0], (((1,), (1,)), ((), ())), preferred_element_type=f32
        ) * HEAD_DIM ** (-0.5)
        scores = scores.reshape(-1, tokens, tokens)
        scores = jnp.where(mask_ref[...][None] > 0.5, scores, -1e30)
        row_max = jnp.max(scores, axis=2, keepdims=True)
        terms = jnp.exp(scores - row_max)
        probs = (terms / jnp.sum(terms, axis=2, keepdims=True)).astype(bf16)
        return jnp.dot(
            probs.reshape(-1, tokens), kv_ref[1], preferred_element_type=f32
        )

    def attend(head, residual):
        return (residual.astype(f32) + mix(queries_ref[head])).astype(bf16)

    def pair_block(source, target):
        return pltpu.make_async_remote_copy(
            src_ref=source,
            dst_ref=target,
            send_sem=pair_sem.at[0],
            recv_sem=pair_sem.at[1],
            device_id=(dp, pipe, pair),
            device_id_type=MESH,
        )

    def stream_copy(head, to_tensor):
        return pltpu.make_async_remote_copy(
            src_ref=first_ref.at[head],
            dst_ref=stream_ref.at[tensor * heads + head],
            send_sem=stream_send.at[head, to_tensor],
            recv_sem=stream_recv.at[tensor * heads + head],
            device_id=(dp, 1, to_tensor),
            device_id_type=MESH,
        )

    weight_exchange = pair_block(gathered.at[0, dp], gathered.at[n_pieces, dp])

    for load in loads_k:
        load.wait()
    lax.fori_loop(0, rows // step_rows, update_k, 0)
    pl.semaphore_wait(barrier, len(near) + 1 + n_tensor)

    direct_pieces = (0, n_pieces - 1)

    @pl.when(pipe == 0)
    def _():
        send(0, True)

    @pl.when(pipe == 1)
    def _():
        weight_exchange.start()

    for load in loads_q:
        load.wait()
    for head in range(heads):
        update_q(head)

        @pl.when(pipe == 0)
        def _():
            send(1 + head, 1 + head in direct_pieces)

    load_x.wait()
    load_seg.wait()

    @pl.when(pipe == 0)
    def _():
        norm(lambda b: x_ref[:, b * HEAD_DIM : (b + 1) * HEAD_DIM].astype(f32))
        tables()
        exchange = pair_block(kv_ref.at[slot], kv_ref.at[slot])
        arrived(0, True)
        block = jnp.dot(normed_ref[...], weights(0), preferred_element_type=f32)
        kv_ref[slot] = key_or_value(block, holds_key)
        exchange.start()
        for p in range(1, n_pieces):
            if p not in direct_pieces:
                relay(p)
        pl.semaphore_signal(
            go_sem, inc=1, device_id=(dp, 1, tensor), device_id_type=MESH
        )
        for n in range(heads):
            head = (n + heads - 1) % heads
            arrived(1 + head, 1 + head in direct_pieces)
            project(head)
            if n == 0:
                exchange.wait()
            columns = pl.ds(
                pl.multiple_of((tensor * heads + head) * HEAD_DIM, HEAD_DIM), HEAD_DIM
            )
            result = attend(head, x_ref[:, columns])
            first_ref[head] = result
            for t in far_first:
                stream_copy(head, t).start()
            out_ref[:, head * HEAD_DIM : (head + 1) * HEAD_DIM] = result
        for p in range(n_pieces):
            all_sent(p, p in direct_pieces)
        for head in range(heads):
            for t in range(n_tensor):
                stream_copy(head, t).wait_send()

    @pl.when(pipe == 1)
    def _():
        tables()
        weight_exchange.wait()
        order = [0, n_pieces] + list(range(1, n_pieces))
        pl.semaphore_wait(go_sem, 1)
        for p in order:
            send(p, False)
        for p in order:
            relay(p)
        for p in order:
            arrived(p, False)

        def stream_arrived(source):
            for head in range(heads):
                pltpu.make_async_remote_copy(
                    src_ref=first_ref.at[head],
                    dst_ref=stream_ref.at[source * heads + head],
                    send_sem=stream_send.at[head, source],
                    recv_sem=stream_recv.at[source * heads + head],
                    device_id=(dp, 0, tensor),
                    device_id_type=MESH,
                ).wait_recv()

        if blockwise:
            squares = jnp.zeros((tokens, HEAD_DIM), f32)
            for n, source in enumerate(reversed(far_first)):
                stream_arrived(source)
                parts = [stream_ref[source * heads + h] for h in range(heads)]
                for part in parts:
                    value = part.astype(f32)
                    squares += value * value
                block = jnp.dot(
                    jnp.concatenate(parts, axis=1),
                    jnp.concatenate([gathered[p, source] for p in order], axis=1),
                    preferred_element_type=f32,
                )
                sums_ref[...] = block if n == 0 else sums_ref[...] + block
            mean = jnp.sum(squares, axis=1, keepdims=True) / features
            scale = lax.rsqrt(mean + norm_eps)

            def projected(n):
                return sums_ref[:, n * HEAD_DIM : (n + 1) * HEAD_DIM] * scale

        else:
            for source in far_first:
                stream_arrived(source)
            norm(lambda b: stream_ref[b].astype(f32))

            def projected(n):
                return jnp.dot(
                    normed_ref[...], weights(order[n]), preferred_element_type=f32
                )

        kv_ref[slot] = key_or_value(projected(0), holds_key)
        kv_ref[1 - slot] = key_or_value(projected(1), jnp.logical_not(holds_key))
        queries = [
            rope(projected(2 + head), cos_ref[...], sin_ref[...]).astype(bf16)
            for head in range(heads)
        ]
        mixed = mix(jnp.concatenate(queries, axis=0))
        for head in range(heads):
            residual = stream_ref[tensor * heads + head].astype(f32)
            out_ref[:, head * HEAD_DIM : (head + 1) * HEAD_DIM] = (
                residual + mixed[head * tokens : (head + 1) * tokens]
            ).astype(bf16)
        for p in order:
            all_sent(p, False)


def sections_call(n_dp, n_tensor, stream, segments, q_arrays, kv_arrays):
    tokens, features = stream.shape
    _, rows, q_cols = q_arrays[0].shape
    kv_cols = kv_arrays[0].shape[2]
    heads = q_cols // HEAD_DIM
    n_pieces = 1 + heads
    kinds = 6 if n_dp == 4 else n_dp - 1
    bf16 = jnp.bfloat16
    f32 = jnp.float32
    vmem = pl.BlockSpec(memory_space=pltpu.VMEM)
    anywhere = pl.BlockSpec(memory_space=pl.ANY)
    return pl.pallas_call(
        functools.partial(sections_kernel, n_dp, n_tensor),
        out_shape=[pltpu.VMEM((1, rows, q_cols), f32)] * 3
        + [pltpu.VMEM((1, rows, kv_cols), f32)] * 3
        + [pltpu.VMEM((tokens, q_cols), bf16)],
        in_specs=[anywhere] * 10,
        out_specs=[vmem] * 7,
        scratch_shapes=[
            pltpu.VMEM((tokens, features), bf16),
            pltpu.VMEM(segments.shape, jnp.int32),
            pltpu.VMEM((4, rows, q_cols), f32),
            pltpu.VMEM((4, rows, kv_cols), f32),
            pltpu.SemaphoreType.DMA((10,)),
            pltpu.VMEM((n_pieces + 1, n_dp, rows, HEAD_DIM), bf16),
            pltpu.VMEM((tokens, features), bf16),
            pltpu.VMEM((tokens, HEAD_DIM), jnp.float32),
            pltpu.VMEM((tokens, HEAD_DIM), jnp.float32),
            pltpu.VMEM((tokens, tokens), jnp.float32),
            pltpu.VMEM((2, tokens, HEAD_DIM), bf16),
            pltpu.VMEM((heads, tokens, HEAD_DIM), bf16),
            pltpu.VMEM((tokens, (n_pieces + 1) * HEAD_DIM), f32),
            pltpu.VMEM((heads, tokens, HEAD_DIM), bf16),
            pltpu.VMEM((n_tensor * heads, tokens, HEAD_DIM), bf16),
            pltpu.SemaphoreType.DMA((n_pieces + 1, kinds)),
            pltpu.SemaphoreType.DMA((n_pieces + 1, kinds)),
            pltpu.SemaphoreType.DMA((2,)),
            pltpu.SemaphoreType.DMA((heads, n_tensor)),
            pltpu.SemaphoreType.DMA((n_tensor * heads,)),
            pltpu.SemaphoreType.REGULAR,
        ],
        compiler_params=pltpu.CompilerParams(collective_id=0, has_side_effects=True),
    )(stream, segments, *q_arrays, *kv_arrays)


def solution(mesh):
    n_dp, n_tensor = mesh.shape["dp"], mesh.shape["tensor"]

    def on_device(
        stream_in,
        segment_ids,
        master_q,
        moment_q,
        second_q,
        grad_q,
        master_kv,
        moment_kv,
        second_kv,
        grad_kv,
    ):
        fresh = sections_call(
            n_dp,
            n_tensor,
            stream_in,
            segment_ids,
            (master_q, moment_q, second_q, grad_q),
            (master_kv, moment_kv, second_kv, grad_kv),
        )
        *states, result = write_call(fresh)
        return (*states, result[None])

    weight_spec = P("pipe", "dp", "tensor")
    return jax.shard_map(
        on_device,
        mesh=mesh,
        in_specs=(P("dp", None), P("dp", None)) + (weight_spec,) * 8,
        out_specs=(weight_spec,) * 7,
        check_vma=False,
    )
```

```python
import functools

import jax
import jax.numpy as jnp
from jax import lax
from jax.experimental import pallas as pl
from jax.experimental.pallas import tpu as pltpu
from jax.sharding import PartitionSpec as P

HEAD_DIM = 128
MESH = pl.DeviceIdType.MESH

beta_one = 0.9
beta_two = 0.999
adam_eps = 1e-08
learn_rate = 0.003
decay_rate = 0.1
adam_step = 10.0
norm_eps = 1e-05


def adamw(master, moment, second, gradient):
    moment_new = beta_one * moment + (1.0 - beta_one) * gradient
    second_new = beta_two * second + (1.0 - beta_two) * gradient * gradient
    fix_one = 1.0 - beta_one**adam_step
    fix_two = 1.0 - beta_two**adam_step
    step_dir = moment_new / fix_one / (jnp.sqrt(second_new / fix_two) + adam_eps)
    master_new = master - learn_rate * (step_dir + decay_rate * master)
    return (master_new, moment_new, second_new)


def write_kernel(*refs):
    count = (len(refs) - 1) // 2
    sems = refs[-1]
    copies = []
    for i in range(count):
        source, target = refs[i], refs[count + i]
        rows = source.shape[-2]
        step = rows // 3 if rows % 24 == 0 and source.dtype == jnp.float32 else rows
        for n in range(rows // step):
            at = (Ellipsis, pl.ds(n * step, step), slice(None))
            copies.append(
                pltpu.make_async_copy(source.at[at], target.at[at], sems.at[i, n])
            )
    for copy in copies:
        copy.start()
    for copy in copies:
        copy.wait()


def write_call(arrays):
    return pl.pallas_call(
        write_kernel,
        in_specs=[pl.BlockSpec(memory_space=pltpu.VMEM)] * len(arrays),
        out_specs=[pl.BlockSpec(memory_space=pl.ANY)] * len(arrays),
        out_shape=[jax.ShapeDtypeStruct(a.shape, a.dtype) for a in arrays],
        scratch_shapes=[pltpu.SemaphoreType.DMA((len(arrays), 3))],
    )(*[pltpu.with_memory_space_constraint(a, pltpu.VMEM) for a in arrays])


def sections_kernel(
    n_dp,
    n_tensor,
    x_hbm,
    seg_hbm,
    mq_hbm,
    eq_hbm,
    sq_hbm,
    gq_hbm,
    mk_hbm,
    ek_hbm,
    sk_hbm,
    gk_hbm,
    nmq,
    neq,
    nsq,
    nmk,
    nek,
    nsk,
    out_ref,
    x_ref,
    seg_ref,
    q_ref,
    k_ref,
    load_sem,
    gathered,
    normed_ref,
    cos_ref,
    sin_ref,
    mask_ref,
    kv_ref,
    queries_ref,
    sums_ref,
    first_ref,
    stream_ref,
    send_sem,
    recv_sem,
    pair_sem,
    stream_send,
    stream_recv,
    go_sem,
):
    dp = lax.axis_index("dp")
    pipe = lax.axis_index("pipe")
    tensor = lax.axis_index("tensor")
    tokens, features = x_ref.shape
    rows = q_ref.shape[1]
    heads = first_ref.shape[0]
    n_pieces = 1 + heads
    half_rows = rows // 2
    relayed = n_dp == 4
    half = n_tensor // 2
    pair = lax.rem(tensor + half, n_tensor)
    holds_key = tensor < half
    slot = jnp.where(holds_key, 0, 1)
    f32 = jnp.float32
    bf16 = jnp.bfloat16

    if n_tensor == 4:
        far_first = [3 - tensor, pair, tensor + 1 - 2 * lax.rem(tensor, 2), tensor]
    else:
        far_first = [lax.rem(tensor + off, n_tensor) for off in range(n_tensor)]
    blockwise = rows == heads * HEAD_DIM and n_dp == n_tensor

    x_side = dp + 1 - 2 * lax.rem(dp, 2)
    y_side = lax.rem(dp + 2, 4)

    barrier = pltpu.get_barrier_semaphore()
    if relayed:
        near = [x_side, y_side, 3 - dp]
    else:
        near = [lax.rem(dp + off, n_dp) for off in range(1, n_dp)]
    for peer in near:
        pl.semaphore_signal(
            barrier, inc=1, device_id=(peer, pipe, tensor), device_id_type=MESH
        )
    pl.semaphore_signal(barrier, inc=1, device_id=(dp, pipe, pair), device_id_type=MESH)
    for t in far_first[1:] if n_tensor == 4 else far_first:
        pl.semaphore_signal(
            barrier, inc=1, device_id=(dp, 1 - pipe, t), device_id_type=MESH
        )

    load_x = pltpu.make_async_copy(x_hbm, x_ref, load_sem.at[8])
    load_seg = pltpu.make_async_copy(seg_hbm, seg_ref, load_sem.at[9])
    loads_k = [
        pltpu.make_async_copy(ref.at[0], k_ref.at[i], load_sem.at[i])
        for i, ref in enumerate((mk_hbm, ek_hbm, sk_hbm, gk_hbm))
    ]
    loads_q = [
        pltpu.make_async_copy(ref.at[0], q_ref.at[i], load_sem.at[4 + i])
        for i, ref in enumerate((mq_hbm, eq_hbm, sq_hbm, gq_hbm))
    ]
    for load in loads_k + loads_q + [load_x, load_seg]:
        load.start()

    def norm(read_block):
        blocks = features // HEAD_DIM
        squares = jnp.zeros((tokens, HEAD_DIM), f32)
        for b in range(blocks):
            value = read_block(b)
            squares += value * value
        mean = jnp.sum(squares, axis=1, keepdims=True) / features
        scale = lax.rsqrt(mean + norm_eps)
        for b in range(blocks):
            normed_ref[:, b * HEAD_DIM : (b + 1) * HEAD_DIM] = (
                read_block(b) * scale
            ).astype(bf16)

    def tables():
        row = lax.broadcasted_iota(jnp.int32, (tokens, tokens), 0)
        col = lax.broadcasted_iota(jnp.int32, (tokens, tokens), 1)
        seg_row = jnp.broadcast_to(seg_ref[...].astype(f32), (tokens, tokens))
        seg_col = jnp.sum(jnp.where(row == col, seg_row, 0.0), axis=1, keepdims=True)
        same = seg_row == seg_col
        mask_ref[...] = jnp.where(same & (col <= row), 1.0, 0.0)
        position = jnp.sum(jnp.where(same & (col < row), 1.0, 0.0), axis=1, keepdims=True)
        lane = lax.broadcasted_iota(jnp.int32, (1, HEAD_DIM), 1)
        half_dim = HEAD_DIM // 2
        index = jnp.where(lane < half_dim, lane, lane - half_dim).astype(f32)
        inverse_freq = 10000.0 ** (-2.0 * index / HEAD_DIM)
        angles = position * inverse_freq
        cos_ref[...] = jnp.cos(angles)
        sine = jnp.sin(angles)
        sin_ref[...] = jnp.where(lane < half_dim, -sine, sine)

    step_rows = 48 if rows % 48 == 0 else rows

    def update_k(i, carry):
        at = pl.ds(pl.multiple_of(i * step_rows, step_rows), step_rows)
        new = adamw(k_ref[0, at], k_ref[1, at], k_ref[2, at], k_ref[3, at])
        nmk[0, at], nek[0, at], nsk[0, at] = new
        gathered[0, dp, at] = new[0].astype(bf16)
        return carry

    def update_q(head):
        columns = slice(head * HEAD_DIM, (head + 1) * HEAD_DIM)

        def step(i, carry):
            at = pl.ds(pl.multiple_of(i * step_rows, step_rows), step_rows)
            new = adamw(*[q_ref[n, at, columns] for n in range(4)])
            nmq[0, at, columns], neq[0, at, columns], nsq[0, at, columns] = new
            gathered[1 + head, dp, at] = new[0].astype(bf16)
            return carry

        lax.fori_loop(0, rows // step_rows, step, 0)

    part_a = pl.ds(0, half_rows)
    part_b = pl.ds(half_rows, half_rows)

    def copy_to(peer, ref, piece, kind):
        return pltpu.make_async_remote_copy(
            src_ref=ref,
            dst_ref=ref,
            send_sem=send_sem.at[piece, kind],
            recv_sem=recv_sem.at[piece, kind],
            device_id=(peer, pipe, tensor),
            device_id_type=MESH,
        )

    def direct_copies(piece):
        own = gathered.at[piece, dp]
        if relayed:
            return [
                copy_to(3 - dp, own, piece, 0),
                copy_to(x_side, own, piece, 1),
                copy_to(y_side, own, piece, 2),
            ]
        return [copy_to(peer, own, piece, n) for n, peer in enumerate(near)]

    def own_copies(piece, kinds=range(4)):
        peers = (x_side, y_side, x_side, y_side)
        parts = (part_a, part_b, part_b, part_a)
        return [
            copy_to(peers[n], gathered.at[piece, dp, parts[n]], piece, n) for n in kinds
        ]

    def relay_copies(piece):
        return [
            copy_to(y_side, gathered.at[piece, x_side, part_a], piece, 4),
            copy_to(x_side, gathered.at[piece, y_side, part_b], piece, 5),
        ]

    def start(copies):
        for copy in copies:
            copy.start()

    def send(piece, direct):
        start(direct_copies(piece) if direct or not relayed else own_copies(piece))

    def relay(piece):
        if not relayed:
            return
        for got, passed in zip(own_copies(piece, (0, 1)), relay_copies(piece)):
            got.wait_recv()
            passed.start()

    def arrived(piece, direct):
        if direct or not relayed:
            copies = direct_copies(piece)
        else:
            copies = own_copies(piece, (2, 3)) + relay_copies(piece)
        for copy in copies:
            copy.wait_recv()

    def all_sent(piece, direct):
        if direct or not relayed:
            copies = direct_copies(piece)
        else:
            copies = own_copies(piece) + relay_copies(piece)
        for copy in copies:
            copy.wait_send()

    def weights(piece):
        return gathered[piece].reshape(n_dp * rows, HEAD_DIM)

    def rope(values, cosine, sine):
        return values * cosine + pltpu.roll(values, HEAD_DIM // 2, 1) * sine

    def key_or_value(values, is_key):
        cosine = jnp.where(is_key, cos_ref[...], 1.0)
        sine = jnp.where(is_key, sin_ref[...], 0.0)
        return rope(values, cosine, sine).astype(bf16)

    def project(head):
        queries = jnp.dot(normed_ref[...], weights(1 + head), preferred_element_type=f32)
        queries_ref[head] = rope(queries, cos_ref[...], sin_ref[...]).astype(bf16)

    def mix(queries):
        scores = lax.dot_general(
            queries, kv_ref[0], (((1,), (1,)), ((), ())), preferred_element_type=f32
        ) * HEAD_DIM ** (-0.5)
        scores = scores.reshape(-1, tokens, tokens)
        scores = jnp.where(mask_ref[...][None] > 0.5, scores, -1e30)
        row_max = jnp.max(scores, axis=2, keepdims=True)
        terms = jnp.exp(scores - row_max)
        probs = (terms / jnp.sum(terms, axis=2, keepdims=True)).astype(bf16)
        return jnp.dot(
            probs.reshape(-1, tokens), kv_ref[1], preferred_element_type=f32
        )

    def attend(head, residual):
        return (residual.astype(f32) + mix(queries_ref[head])).astype(bf16)

    def pair_block(source, target):
        return pltpu.make_async_remote_copy(
            src_ref=source,
            dst_ref=target,
            send_sem=pair_sem.at[0],
            recv_sem=pair_sem.at[1],
            device_id=(dp, pipe, pair),
            device_id_type=MESH,
        )

    def stream_copy(head, to_tensor):
        return pltpu.make_async_remote_copy(
            src_ref=first_ref.at[head],
            dst_ref=stream_ref.at[tensor * heads + head],
            send_sem=stream_send.at[head, to_tensor],
            recv_sem=stream_recv.at[tensor * heads + head],
            device_id=(dp, 1, to_tensor),
            device_id_type=MESH,
        )

    weight_exchange = pair_block(gathered.at[0, dp], gathered.at[n_pieces, dp])

    for load in loads_k:
        load.wait()
    lax.fori_loop(0, rows // step_rows, update_k, 0)
    pl.semaphore_wait(barrier, len(near) + 1 + n_tensor - (n_tensor == 4))

    direct_pieces = (0, 1)

    @pl.when(pipe == 0)
    def _():
        send(0, True)

    @pl.when(pipe == 1)
    def _():
        weight_exchange.start()

    for load in loads_q:
        load.wait()
    for head in range(heads):
        update_q(head)

        @pl.when(pipe == 0)
        def _():
            send(1 + head, 1 + head in direct_pieces)

    load_x.wait()
    load_seg.wait()

    @pl.when(pipe == 0)
    def _():
        norm(lambda b: x_ref[:, b * HEAD_DIM : (b + 1) * HEAD_DIM].astype(f32))
        tables()
        exchange = pair_block(kv_ref.at[slot], kv_ref.at[slot])
        arrived(0, True)
        block = jnp.dot(normed_ref[...], weights(0), preferred_element_type=f32)
        kv_ref[slot] = key_or_value(block, holds_key)
        exchange.start()
        pl.semaphore_signal(
            go_sem, inc=1, device_id=(dp, 1, tensor), device_id_type=MESH
        )
        for head in range(heads):
            arrived(1 + head, 1 + head in direct_pieces)
            project(head)
            if head == 0:
                for p in range(2, n_pieces):
                    relay(p)
                exchange.wait()
            columns = pl.ds(
                pl.multiple_of((tensor * heads + head) * HEAD_DIM, HEAD_DIM), HEAD_DIM
            )
            result = attend(head, x_ref[:, columns])
            first_ref[head] = result
            for t in far_first:
                stream_copy(head, t).start()
            out_ref[:, head * HEAD_DIM : (head + 1) * HEAD_DIM] = result
        for p in range(n_pieces):
            all_sent(p, p in direct_pieces)
        for head in range(heads):
            for t in range(n_tensor):
                stream_copy(head, t).wait_send()

    @pl.when(pipe == 1)
    def _():
        tables()
        weight_exchange.wait()
        order = [0, n_pieces] + list(range(1, n_pieces))
        pl.semaphore_wait(go_sem, 1)
        for p in order:
            send(p, False)
        for p in order:
            relay(p)
        for p in order[:-1] if blockwise else order:
            arrived(p, False)

        def stream_arrived(source):
            for head in range(heads):
                pltpu.make_async_remote_copy(
                    src_ref=first_ref.at[head],
                    dst_ref=stream_ref.at[source * heads + head],
                    send_sem=stream_send.at[head, source],
                    recv_sem=stream_recv.at[source * heads + head],
                    device_id=(dp, 0, tensor),
                    device_id_type=MESH,
                ).wait_recv()

        if blockwise:
            sources = far_first[::-1]
            split = (n_pieces) * HEAD_DIM

            def source_block(source):
                return jnp.concatenate(
                    [stream_ref[source * heads + h] for h in range(heads)], axis=1
                )

            def product(source, pieces):
                return jnp.dot(
                    source_block(source),
                    jnp.concatenate([gathered[p, source] for p in pieces], axis=1),
                    preferred_element_type=f32,
                )

            def add_squares(source, squares):
                for h in range(heads):
                    value = stream_ref[source * heads + h].astype(f32)
                    squares += value * value
                return squares

            squares = jnp.zeros((tokens, HEAD_DIM), f32)
            for n, source in enumerate(sources[:-1]):
                stream_arrived(source)
                squares = add_squares(source, squares)
                block = product(source, order[:-1])
                if n == 0:
                    sums_ref[:, :split] = block
                else:
                    sums_ref[:, :split] += block
            arrived(order[-1], False)
            block = product(sources[0], order[-1:])
            for source in sources[1:-1]:
                block += product(source, order[-1:])
            sums_ref[:, split:] = block
            stream_arrived(sources[-1])
            squares = add_squares(sources[-1], squares)
            sums_ref[...] += product(sources[-1], order)
            mean = jnp.sum(squares, axis=1, keepdims=True) / features
            scale = lax.rsqrt(mean + norm_eps)

            def projected(n):
                return sums_ref[:, n * HEAD_DIM : (n + 1) * HEAD_DIM] * scale

        else:
            for source in far_first:
                stream_arrived(source)
            norm(lambda b: stream_ref[b].astype(f32))

            def projected(n):
                return jnp.dot(
                    normed_ref[...], weights(order[n]), preferred_element_type=f32
                )

        kv_ref[slot] = key_or_value(projected(0), holds_key)
        kv_ref[1 - slot] = key_or_value(projected(1), jnp.logical_not(holds_key))
        queries = [
            rope(projected(2 + head), cos_ref[...], sin_ref[...]).astype(bf16)
            for head in range(heads)
        ]
        mixed = mix(jnp.concatenate(queries, axis=0))
        for head in range(heads):
            residual = stream_ref[tensor * heads + head].astype(f32)
            out_ref[:, head * HEAD_DIM : (head + 1) * HEAD_DIM] = (
                residual + mixed[head * tokens : (head + 1) * tokens]
            ).astype(bf16)
        for p in order:
            all_sent(p, False)


def sections_call(n_dp, n_tensor, stream, segments, q_arrays, kv_arrays):
    tokens, features = stream.shape
    _, rows, q_cols = q_arrays[0].shape
    kv_cols = kv_arrays[0].shape[2]
    heads = q_cols // HEAD_DIM
    n_pieces = 1 + heads
    kinds = 6 if n_dp == 4 else n_dp - 1
    bf16 = jnp.bfloat16
    f32 = jnp.float32
    vmem = pl.BlockSpec(memory_space=pltpu.VMEM)
    anywhere = pl.BlockSpec(memory_space=pl.ANY)
    return pl.pallas_call(
        functools.partial(sections_kernel, n_dp, n_tensor),
        out_shape=[pltpu.VMEM((1, rows, q_cols), f32)] * 3
        + [pltpu.VMEM((1, rows, kv_cols), f32)] * 3
        + [pltpu.VMEM((tokens, q_cols), bf16)],
        in_specs=[anywhere] * 10,
        out_specs=[vmem] * 7,
        scratch_shapes=[
            pltpu.VMEM((tokens, features), bf16),
            pltpu.VMEM(segments.shape, jnp.int32),
            pltpu.VMEM((4, rows, q_cols), f32),
            pltpu.VMEM((4, rows, kv_cols), f32),
            pltpu.SemaphoreType.DMA((10,)),
            pltpu.VMEM((n_pieces + 1, n_dp, rows, HEAD_DIM), bf16),
            pltpu.VMEM((tokens, features), bf16),
            pltpu.VMEM((tokens, HEAD_DIM), jnp.float32),
            pltpu.VMEM((tokens, HEAD_DIM), jnp.float32),
            pltpu.VMEM((tokens, tokens), jnp.float32),
            pltpu.VMEM((2, tokens, HEAD_DIM), bf16),
            pltpu.VMEM((heads, tokens, HEAD_DIM), bf16),
            pltpu.VMEM((tokens, (n_pieces + 1) * HEAD_DIM), f32),
            pltpu.VMEM((heads, tokens, HEAD_DIM), bf16),
            pltpu.VMEM((n_tensor * heads, tokens, HEAD_DIM), bf16),
            pltpu.SemaphoreType.DMA((n_pieces + 1, kinds)),
            pltpu.SemaphoreType.DMA((n_pieces + 1, kinds)),
            pltpu.SemaphoreType.DMA((2,)),
            pltpu.SemaphoreType.DMA((heads, n_tensor)),
            pltpu.SemaphoreType.DMA((n_tensor * heads,)),
            pltpu.SemaphoreType.REGULAR,
        ],
        compiler_params=pltpu.CompilerParams(collective_id=0, has_side_effects=True),
    )(stream, segments, *q_arrays, *kv_arrays)


def solution(mesh):
    n_dp, n_tensor = mesh.shape["dp"], mesh.shape["tensor"]

    def on_device(
        stream_in,
        segment_ids,
        master_q,
        moment_q,
        second_q,
        grad_q,
        master_kv,
        moment_kv,
        second_kv,
        grad_kv,
    ):
        fresh = sections_call(
            n_dp,
            n_tensor,
            stream_in,
            segment_ids,
            (master_q, moment_q, second_q, grad_q),
            (master_kv, moment_kv, second_kv, grad_kv),
        )
        *states, result = write_call(fresh)
        return (*states, result[None])

    weight_spec = P("pipe", "dp", "tensor")
    return jax.shard_map(
        on_device,
        mesh=mesh,
        in_specs=(P("dp", None), P("dp", None)) + (weight_spec,) * 8,
        out_specs=(weight_spec,) * 7,
        check_vma=False,
    )
```

```python
import functools

import jax
import jax.numpy as jnp
from jax import lax
from jax.experimental import pallas as pl
from jax.experimental.pallas import tpu as pltpu
from jax.sharding import PartitionSpec as P

HEAD_DIM = 128
MESH = pl.DeviceIdType.MESH

beta_one = 0.9
beta_two = 0.999
adam_eps = 1e-08
learn_rate = 0.003
decay_rate = 0.1
adam_step = 10.0
norm_eps = 1e-05


def adamw(master, moment, second, gradient):
    moment_new = beta_one * moment + (1.0 - beta_one) * gradient
    second_new = beta_two * second + (1.0 - beta_two) * gradient * gradient
    fix_one = 1.0 - beta_one**adam_step
    fix_two = 1.0 - beta_two**adam_step
    step_dir = moment_new / fix_one / (jnp.sqrt(second_new / fix_two) + adam_eps)
    master_new = master - learn_rate * (step_dir + decay_rate * master)
    return (master_new, moment_new, second_new)


def write_kernel(*refs):
    count = (len(refs) - 1) // 2
    sems = refs[-1]
    copies = [
        pltpu.make_async_copy(refs[i], refs[count + i], sems.at[i]) for i in range(count)
    ]
    for copy in copies:
        copy.start()
    for copy in copies:
        copy.wait()


def write_call(arrays):
    return pl.pallas_call(
        write_kernel,
        in_specs=[pl.BlockSpec(memory_space=pl.ANY)] * len(arrays),
        out_specs=[pl.BlockSpec(memory_space=pl.ANY)] * len(arrays),
        out_shape=[jax.ShapeDtypeStruct(a.shape, a.dtype) for a in arrays],
        scratch_shapes=[pltpu.SemaphoreType.DMA((len(arrays),))],
    )(*[pltpu.with_memory_space_constraint(a, pltpu.VMEM) for a in arrays])


def sections_kernel(
    n_dp,
    n_tensor,
    x_hbm,
    seg_hbm,
    mq_hbm,
    eq_hbm,
    sq_hbm,
    gq_hbm,
    mk_hbm,
    ek_hbm,
    sk_hbm,
    gk_hbm,
    nmq,
    neq,
    nsq,
    nmk,
    nek,
    nsk,
    out_ref,
    x_ref,
    seg_ref,
    q_ref,
    k_ref,
    load_sem,
    gathered,
    normed_ref,
    cos_ref,
    sin_ref,
    mask_ref,
    kv_ref,
    queries_ref,
    sums_ref,
    first_ref,
    stream_ref,
    send_sem,
    recv_sem,
    pair_sem,
    stream_send,
    stream_recv,
    go_sem,
):
    dp = lax.axis_index("dp")
    pipe = lax.axis_index("pipe")
    tensor = lax.axis_index("tensor")
    tokens, features = x_ref.shape
    rows = q_ref.shape[1]
    heads = first_ref.shape[0]
    n_pieces = 1 + heads
    half_rows = rows // 2
    relayed = n_dp == 4
    half = n_tensor // 2
    pair = lax.rem(tensor + half, n_tensor)
    holds_key = tensor < half
    slot = jnp.where(holds_key, 0, 1)
    f32 = jnp.float32
    bf16 = jnp.bfloat16

    if n_tensor == 4:
        far_first = [3 - tensor, pair, tensor + 1 - 2 * lax.rem(tensor, 2), tensor]
    else:
        far_first = [lax.rem(tensor + off, n_tensor) for off in range(n_tensor)]
    blockwise = rows == heads * HEAD_DIM and n_dp == n_tensor

    x_side = dp + 1 - 2 * lax.rem(dp, 2)
    y_side = lax.rem(dp + 2, 4)

    barrier = pltpu.get_barrier_semaphore()
    if relayed:
        near = [x_side, y_side, 3 - dp]
    else:
        near = [lax.rem(dp + off, n_dp) for off in range(1, n_dp)]
    for peer in near:
        pl.semaphore_signal(
            barrier, inc=1, device_id=(peer, pipe, tensor), device_id_type=MESH
        )
    pl.semaphore_signal(barrier, inc=1, device_id=(dp, pipe, pair), device_id_type=MESH)
    for t in far_first[1:] if n_tensor == 4 else far_first:
        pl.semaphore_signal(
            barrier, inc=1, device_id=(dp, 1 - pipe, t), device_id_type=MESH
        )

    load_x = pltpu.make_async_copy(x_hbm, x_ref, load_sem.at[8])
    load_seg = pltpu.make_async_copy(seg_hbm, seg_ref, load_sem.at[9])
    loads_k = [
        pltpu.make_async_copy(ref.at[0], k_ref.at[i], load_sem.at[i])
        for i, ref in enumerate((mk_hbm, ek_hbm, sk_hbm, gk_hbm))
    ]
    loads_q = [
        pltpu.make_async_copy(ref.at[0], q_ref.at[i], load_sem.at[4 + i])
        for i, ref in enumerate((mq_hbm, eq_hbm, sq_hbm, gq_hbm))
    ]
    for load in loads_k + loads_q + [load_x, load_seg]:
        load.start()

    def norm(read_block):
        blocks = features // HEAD_DIM
        squares = jnp.zeros((tokens, HEAD_DIM), f32)
        for b in range(blocks):
            value = read_block(b)
            squares += value * value
        mean = jnp.sum(squares, axis=1, keepdims=True) / features
        scale = lax.rsqrt(mean + norm_eps)
        for b in range(blocks):
            normed_ref[:, b * HEAD_DIM : (b + 1) * HEAD_DIM] = (
                read_block(b) * scale
            ).astype(bf16)

    def tables():
        row = lax.broadcasted_iota(jnp.int32, (tokens, tokens), 0)
        col = lax.broadcasted_iota(jnp.int32, (tokens, tokens), 1)
        seg_row = jnp.broadcast_to(seg_ref[...].astype(f32), (tokens, tokens))
        seg_col = jnp.sum(jnp.where(row == col, seg_row, 0.0), axis=1, keepdims=True)
        same = seg_row == seg_col
        mask_ref[...] = jnp.where(same & (col <= row), 1.0, 0.0)
        position = jnp.sum(jnp.where(same & (col < row), 1.0, 0.0), axis=1, keepdims=True)
        lane = lax.broadcasted_iota(jnp.int32, (1, HEAD_DIM), 1)
        half_dim = HEAD_DIM // 2
        index = jnp.where(lane < half_dim, lane, lane - half_dim).astype(f32)
        inverse_freq = 10000.0 ** (-2.0 * index / HEAD_DIM)
        angles = position * inverse_freq
        cos_ref[...] = jnp.cos(angles)
        sine = jnp.sin(angles)
        sin_ref[...] = jnp.where(lane < half_dim, -sine, sine)

    step_rows = 48 if rows % 48 == 0 else rows

    def update_k(i, carry):
        at = pl.ds(pl.multiple_of(i * step_rows, step_rows), step_rows)
        new = adamw(k_ref[0, at], k_ref[1, at], k_ref[2, at], k_ref[3, at])
        k_ref[0, at], k_ref[1, at], k_ref[2, at] = new
        gathered[0, dp, at] = new[0].astype(bf16)
        return carry

    def update_q(head):
        columns = slice(head * HEAD_DIM, (head + 1) * HEAD_DIM)

        def step(i, carry):
            at = pl.ds(pl.multiple_of(i * step_rows, step_rows), step_rows)
            new = adamw(*[q_ref[n, at, columns] for n in range(4)])
            q_ref[0, at, columns], q_ref[1, at, columns], q_ref[2, at, columns] = new
            gathered[1 + head, dp, at] = new[0].astype(bf16)
            return carry

        lax.fori_loop(0, rows // step_rows, step, 0)

    part_a = pl.ds(0, half_rows)
    part_b = pl.ds(half_rows, half_rows)

    def copy_to(peer, ref, piece, kind):
        return pltpu.make_async_remote_copy(
            src_ref=ref,
            dst_ref=ref,
            send_sem=send_sem.at[piece, kind],
            recv_sem=recv_sem.at[piece, kind],
            device_id=(peer, pipe, tensor),
            device_id_type=MESH,
        )

    def direct_copies(piece):
        own = gathered.at[piece, dp]
        if relayed:
            return [
                copy_to(3 - dp, own, piece, 0),
                copy_to(x_side, own, piece, 1),
                copy_to(y_side, own, piece, 2),
            ]
        return [copy_to(peer, own, piece, n) for n, peer in enumerate(near)]

    def own_copies(piece, kinds=range(4)):
        peers = (x_side, y_side, x_side, y_side)
        parts = (part_a, part_b, part_b, part_a)
        return [
            copy_to(peers[n], gathered.at[piece, dp, parts[n]], piece, n) for n in kinds
        ]

    def relay_copies(piece):
        return [
            copy_to(y_side, gathered.at[piece, x_side, part_a], piece, 4),
            copy_to(x_side, gathered.at[piece, y_side, part_b], piece, 5),
        ]

    def start(copies):
        for copy in copies:
            copy.start()

    def send(piece, direct):
        start(direct_copies(piece) if direct or not relayed else own_copies(piece))

    def relay(piece):
        if not relayed:
            return
        for got, passed in zip(own_copies(piece, (0, 1)), relay_copies(piece)):
            got.wait_recv()
            passed.start()

    def arrived(piece, direct):
        if direct or not relayed:
            copies = direct_copies(piece)
        else:
            copies = own_copies(piece, (2, 3)) + relay_copies(piece)
        for copy in copies:
            copy.wait_recv()

    def all_sent(piece, direct):
        if direct or not relayed:
            copies = direct_copies(piece)
        else:
            copies = own_copies(piece) + relay_copies(piece)
        for copy in copies:
            copy.wait_send()

    def weights(piece):
        return gathered[piece].reshape(n_dp * rows, HEAD_DIM)

    def rope(values, cosine, sine):
        return values * cosine + pltpu.roll(values, HEAD_DIM // 2, 1) * sine

    def key_or_value(values, is_key):
        cosine = jnp.where(is_key, cos_ref[...], 1.0)
        sine = jnp.where(is_key, sin_ref[...], 0.0)
        return rope(values, cosine, sine).astype(bf16)

    def project(head):
        queries = jnp.dot(normed_ref[...], weights(1 + head), preferred_element_type=f32)
        queries_ref[head] = rope(queries, cos_ref[...], sin_ref[...]).astype(bf16)

    def mix(queries):
        scores = lax.dot_general(
            queries, kv_ref[0], (((1,), (1,)), ((), ())), preferred_element_type=f32
        ) * HEAD_DIM ** (-0.5)
        scores = scores.reshape(-1, tokens, tokens)
        scores = jnp.where(mask_ref[...][None] > 0.5, scores, -1e30)
        row_max = jnp.max(scores, axis=2, keepdims=True)
        terms = jnp.exp(scores - row_max)
        probs = (terms / jnp.sum(terms, axis=2, keepdims=True)).astype(bf16)
        return jnp.dot(
            probs.reshape(-1, tokens), kv_ref[1], preferred_element_type=f32
        )

    def attend(head, residual):
        return (residual.astype(f32) + mix(queries_ref[head])).astype(bf16)

    def pair_block(source, target):
        return pltpu.make_async_remote_copy(
            src_ref=source,
            dst_ref=target,
            send_sem=pair_sem.at[0],
            recv_sem=pair_sem.at[1],
            device_id=(dp, pipe, pair),
            device_id_type=MESH,
        )

    def stream_copy(head, to_tensor):
        return pltpu.make_async_remote_copy(
            src_ref=first_ref.at[head],
            dst_ref=stream_ref.at[tensor * heads + head],
            send_sem=stream_send.at[head, to_tensor],
            recv_sem=stream_recv.at[tensor * heads + head],
            device_id=(dp, 1, to_tensor),
            device_id_type=MESH,
        )

    weight_exchange = pair_block(gathered.at[0, dp], gathered.at[n_pieces, dp])

    for load in loads_k:
        load.wait()
    lax.fori_loop(0, rows // step_rows, update_k, 0)
    pl.semaphore_wait(barrier, len(near) + 1 + n_tensor - (n_tensor == 4))

    direct_pieces = (0, n_pieces - 1)

    @pl.when(pipe == 0)
    def _():
        send(0, True)

    @pl.when(pipe == 1)
    def _():
        weight_exchange.start()

    for load in loads_q:
        load.wait()
    for head in range(heads):
        update_q(head)

        @pl.when(pipe == 0)
        def _():
            send(1 + head, 1 + head in direct_pieces)

    keeps = [
        pltpu.make_async_copy(ref.at[n], out.at[0], load_sem.at[4 * m + n])
        for m, (ref, outs) in enumerate(((k_ref, (nmk, nek, nsk)), (q_ref, (nmq, neq, nsq))))
        for n, out in enumerate(outs)
    ]
    start(keeps)
    load_x.wait()
    load_seg.wait()

    @pl.when(pipe == 0)
    def _():
        norm(lambda b: x_ref[:, b * HEAD_DIM : (b + 1) * HEAD_DIM].astype(f32))
        tables()
        exchange = pair_block(kv_ref.at[slot], kv_ref.at[slot])
        arrived(0, True)
        block = jnp.dot(normed_ref[...], weights(0), preferred_element_type=f32)
        kv_ref[slot] = key_or_value(block, holds_key)
        exchange.start()
        for p in range(1, n_pieces):
            if p not in direct_pieces:
                relay(p)
        pl.semaphore_signal(
            go_sem, inc=1, device_id=(dp, 1, tensor), device_id_type=MESH
        )
        for n in range(heads):
            head = (n + heads - 1) % heads
            arrived(1 + head, 1 + head in direct_pieces)
            project(head)
            if n == 0:
                exchange.wait()
            columns = pl.ds(
                pl.multiple_of((tensor * heads + head) * HEAD_DIM, HEAD_DIM), HEAD_DIM
            )
            result = attend(head, x_ref[:, columns])
            first_ref[head] = result
            for t in far_first:
                stream_copy(head, t).start()
            out_ref[:, head * HEAD_DIM : (head + 1) * HEAD_DIM] = result
        for p in range(n_pieces):
            all_sent(p, p in direct_pieces)
        for head in range(heads):
            for t in range(n_tensor):
                stream_copy(head, t).wait_send()
        for keep in keeps:
            keep.wait()

    @pl.when(pipe == 1)
    def _():
        tables()
        weight_exchange.wait()
        order = [0, n_pieces] + list(range(1, n_pieces))
        pl.semaphore_wait(go_sem, 1)
        for p in order:
            send(p, False)
        for p in order:
            relay(p)
        for p in order[:-1] if blockwise else order:
            arrived(p, False)

        def stream_arrived(source):
            for head in range(heads):
                pltpu.make_async_remote_copy(
                    src_ref=first_ref.at[head],
                    dst_ref=stream_ref.at[source * heads + head],
                    send_sem=stream_send.at[head, source],
                    recv_sem=stream_recv.at[source * heads + head],
                    device_id=(dp, 0, tensor),
                    device_id_type=MESH,
                ).wait_recv()

        if blockwise:
            sources = far_first[::-1]
            split = (n_pieces) * HEAD_DIM

            def source_block(source):
                return jnp.concatenate(
                    [stream_ref[source * heads + h] for h in range(heads)], axis=1
                )

            def product(source, pieces):
                return jnp.dot(
                    source_block(source),
                    jnp.concatenate([gathered[p, source] for p in pieces], axis=1),
                    preferred_element_type=f32,
                )

            def add_squares(source, squares):
                for h in range(heads):
                    value = stream_ref[source * heads + h].astype(f32)
                    squares += value * value
                return squares

            squares = jnp.zeros((tokens, HEAD_DIM), f32)
            for n, source in enumerate(sources[:-1]):
                stream_arrived(source)
                squares = add_squares(source, squares)
                block = product(source, order[:-1])
                if n == 0:
                    sums_ref[:, :split] = block
                else:
                    sums_ref[:, :split] += block
            arrived(order[-1], False)
            block = product(sources[0], order[-1:])
            for source in sources[1:-1]:
                block += product(source, order[-1:])
            sums_ref[:, split:] = block
            stream_arrived(sources[-1])
            squares = add_squares(sources[-1], squares)
            sums_ref[...] += product(sources[-1], order)
            mean = jnp.sum(squares, axis=1, keepdims=True) / features
            scale = lax.rsqrt(mean + norm_eps)

            def projected(n):
                return sums_ref[:, n * HEAD_DIM : (n + 1) * HEAD_DIM] * scale

        else:
            for source in far_first:
                stream_arrived(source)
            norm(lambda b: stream_ref[b].astype(f32))

            def projected(n):
                return jnp.dot(
                    normed_ref[...], weights(order[n]), preferred_element_type=f32
                )

        kv_ref[slot] = key_or_value(projected(0), holds_key)
        kv_ref[1 - slot] = key_or_value(projected(1), jnp.logical_not(holds_key))
        queries = [
            rope(projected(2 + head), cos_ref[...], sin_ref[...]).astype(bf16)
            for head in range(heads)
        ]
        mixed = mix(jnp.concatenate(queries, axis=0))
        for head in range(heads):
            residual = stream_ref[tensor * heads + head].astype(f32)
            out_ref[:, head * HEAD_DIM : (head + 1) * HEAD_DIM] = (
                residual + mixed[head * tokens : (head + 1) * tokens]
            ).astype(bf16)
        for p in order:
            all_sent(p, False)
        for keep in keeps:
            keep.wait()


def sections_call(n_dp, n_tensor, stream, segments, q_arrays, kv_arrays):
    tokens, features = stream.shape
    _, rows, q_cols = q_arrays[0].shape
    kv_cols = kv_arrays[0].shape[2]
    heads = q_cols // HEAD_DIM
    n_pieces = 1 + heads
    kinds = 6 if n_dp == 4 else n_dp - 1
    bf16 = jnp.bfloat16
    f32 = jnp.float32
    vmem = pl.BlockSpec(memory_space=pltpu.VMEM)
    anywhere = pl.BlockSpec(memory_space=pl.ANY)
    return pl.pallas_call(
        functools.partial(sections_kernel, n_dp, n_tensor),
        out_shape=[pltpu.VMEM((1, rows, q_cols), f32)] * 3
        + [pltpu.VMEM((1, rows, kv_cols), f32)] * 3
        + [pltpu.VMEM((tokens, q_cols), bf16)],
        in_specs=[anywhere] * 10,
        out_specs=[anywhere] * 6 + [vmem],
        scratch_shapes=[
            pltpu.VMEM((tokens, features), bf16),
            pltpu.VMEM(segments.shape, jnp.int32),
            pltpu.VMEM((4, rows, q_cols), f32),
            pltpu.VMEM((4, rows, kv_cols), f32),
            pltpu.SemaphoreType.DMA((10,)),
            pltpu.VMEM((n_pieces + 1, n_dp, rows, HEAD_DIM), bf16),
            pltpu.VMEM((tokens, features), bf16),
            pltpu.VMEM((tokens, HEAD_DIM), jnp.float32),
            pltpu.VMEM((tokens, HEAD_DIM), jnp.float32),
            pltpu.VMEM((tokens, tokens), jnp.float32),
            pltpu.VMEM((2, tokens, HEAD_DIM), bf16),
            pltpu.VMEM((heads, tokens, HEAD_DIM), bf16),
            pltpu.VMEM((tokens, (n_pieces + 1) * HEAD_DIM), f32),
            pltpu.VMEM((heads, tokens, HEAD_DIM), bf16),
            pltpu.VMEM((n_tensor * heads, tokens, HEAD_DIM), bf16),
            pltpu.SemaphoreType.DMA((n_pieces + 1, kinds)),
            pltpu.SemaphoreType.DMA((n_pieces + 1, kinds)),
            pltpu.SemaphoreType.DMA((2,)),
            pltpu.SemaphoreType.DMA((heads, n_tensor)),
            pltpu.SemaphoreType.DMA((n_tensor * heads,)),
            pltpu.SemaphoreType.REGULAR,
        ],
        compiler_params=pltpu.CompilerParams(collective_id=0, has_side_effects=True),
    )(stream, segments, *q_arrays, *kv_arrays)


def solution(mesh):
    n_dp, n_tensor = mesh.shape["dp"], mesh.shape["tensor"]

    def on_device(
        stream_in,
        segment_ids,
        master_q,
        moment_q,
        second_q,
        grad_q,
        master_kv,
        moment_kv,
        second_kv,
        grad_kv,
    ):
        fresh = sections_call(
            n_dp,
            n_tensor,
            stream_in,
            segment_ids,
            (master_q, moment_q, second_q, grad_q),
            (master_kv, moment_kv, second_kv, grad_kv),
        )
        *states, result = write_call(fresh)
        return (*states, result[None])

    weight_spec = P("pipe", "dp", "tensor")
    return jax.shard_map(
        on_device,
        mesh=mesh,
        in_specs=(P("dp", None), P("dp", None)) + (weight_spec,) * 8,
        out_specs=(weight_spec,) * 7,
        check_vma=False,
    )
```

```python
import functools

import jax
import jax.numpy as jnp
from jax import lax
from jax.experimental import pallas as pl
from jax.experimental.pallas import tpu as pltpu
from jax.sharding import PartitionSpec as P

HEAD_DIM = 128
MESH = pl.DeviceIdType.MESH

beta_one = 0.9
beta_two = 0.999
adam_eps = 1e-08
learn_rate = 0.003
decay_rate = 0.1
adam_step = 10.0
norm_eps = 1e-05


def adamw(master, moment, second, gradient):
    moment_new = beta_one * moment + (1.0 - beta_one) * gradient
    second_new = beta_two * second + (1.0 - beta_two) * gradient * gradient
    fix_one = 1.0 - beta_one**adam_step
    fix_two = 1.0 - beta_two**adam_step
    step_dir = moment_new / fix_one / (jnp.sqrt(second_new / fix_two) + adam_eps)
    master_new = master - learn_rate * (step_dir + decay_rate * master)
    return (master_new, moment_new, second_new)


def write_kernel(*refs):
    count = (len(refs) - 1) // 2
    sems = refs[-1]
    copies = [
        pltpu.make_async_copy(refs[i], refs[count + i], sems.at[i]) for i in range(count)
    ]
    for copy in copies:
        copy.start()
    for copy in copies:
        copy.wait()


def write_call(arrays):
    return pl.pallas_call(
        write_kernel,
        in_specs=[pl.BlockSpec(memory_space=pltpu.VMEM)] * len(arrays),
        out_specs=[pl.BlockSpec(memory_space=pl.ANY)] * len(arrays),
        out_shape=[jax.ShapeDtypeStruct(a.shape, a.dtype) for a in arrays],
        scratch_shapes=[pltpu.SemaphoreType.DMA((len(arrays),))],
    )(*[pltpu.with_memory_space_constraint(a, pltpu.VMEM) for a in arrays])


def sections_kernel(
    n_dp,
    n_tensor,
    x_hbm,
    seg_hbm,
    mq_hbm,
    eq_hbm,
    sq_hbm,
    gq_hbm,
    mk_hbm,
    ek_hbm,
    sk_hbm,
    gk_hbm,
    nmq,
    neq,
    nsq,
    nmk,
    nek,
    nsk,
    out_ref,
    x_ref,
    seg_ref,
    q_ref,
    k_ref,
    load_sem,
    gathered,
    normed_ref,
    cos_ref,
    sin_ref,
    mask_ref,
    kv_ref,
    queries_ref,
    sums_ref,
    first_ref,
    stream_ref,
    send_sem,
    recv_sem,
    pair_sem,
    stream_recv,
    go_sem,
):
    dp = lax.axis_index("dp")
    pipe = lax.axis_index("pipe")
    tensor = lax.axis_index("tensor")
    tokens, features = x_ref.shape
    rows = q_ref.shape[1]
    heads = first_ref.shape[0]
    n_pieces = 1 + heads
    half_rows = rows // 2
    relayed = n_dp == 4
    half = n_tensor // 2
    pair = lax.rem(tensor + half, n_tensor)
    holds_key = tensor < half
    slot = jnp.where(holds_key, 0, 1)
    f32 = jnp.float32
    bf16 = jnp.bfloat16

    if n_tensor == 4:
        far_first = [3 - tensor, pair, tensor + 1 - 2 * lax.rem(tensor, 2), tensor]
    else:
        far_first = [lax.rem(tensor + off, n_tensor) for off in range(n_tensor)]
    blockwise = rows == heads * HEAD_DIM and n_dp == n_tensor

    x_side = dp + 1 - 2 * lax.rem(dp, 2)
    y_side = lax.rem(dp + 2, n_dp)

    barrier = pltpu.get_barrier_semaphore()
    if relayed:
        near = [x_side, y_side, 3 - dp]
    else:
        near = [lax.rem(dp + off, n_dp) for off in range(1, n_dp)]
    for peer in near:
        pl.semaphore_signal(
            barrier, inc=1, device_id=(peer, pipe, tensor), device_id_type=MESH
        )
    pl.semaphore_signal(barrier, inc=1, device_id=(dp, pipe, pair), device_id_type=MESH)
    for t in far_first[1:] if n_tensor == 4 else far_first:
        pl.semaphore_signal(
            barrier, inc=1, device_id=(dp, 1 - pipe, t), device_id_type=MESH
        )

    load_x = pltpu.make_async_copy(x_hbm, x_ref, load_sem.at[2])
    load_seg = pltpu.make_async_copy(seg_hbm, seg_ref, load_sem.at[3])
    for n, ref in enumerate((mk_hbm, ek_hbm, sk_hbm, gk_hbm)):
        pltpu.make_async_copy(ref.at[0], k_ref.at[n], load_sem.at[0]).start()
    for n, ref in enumerate((mq_hbm, eq_hbm, sq_hbm, gq_hbm)):
        pltpu.make_async_copy(ref.at[0], q_ref.at[n], load_sem.at[1]).start()
    load_x.start()
    load_seg.start()

    def norm(read_block):
        blocks = features // HEAD_DIM
        squares = jnp.zeros((tokens, HEAD_DIM), f32)
        for b in range(blocks):
            value = read_block(b)
            squares += value * value
        mean = jnp.sum(squares, axis=1, keepdims=True) / features
        scale = lax.rsqrt(mean + norm_eps)
        for b in range(blocks):
            normed_ref[:, b * HEAD_DIM : (b + 1) * HEAD_DIM] = (
                read_block(b) * scale
            ).astype(bf16)

    def tables():
        row = lax.broadcasted_iota(jnp.int32, (tokens, tokens), 0)
        col = lax.broadcasted_iota(jnp.int32, (tokens, tokens), 1)
        seg_row = jnp.broadcast_to(seg_ref[...].astype(f32), (tokens, tokens))
        seg_col = jnp.sum(jnp.where(row == col, seg_row, 0.0), axis=1, keepdims=True)
        same = seg_row == seg_col
        mask_ref[...] = jnp.where(same & (col <= row), 1.0, 0.0)
        position = jnp.sum(jnp.where(same & (col < row), 1.0, 0.0), axis=1, keepdims=True)
        lane = lax.broadcasted_iota(jnp.int32, (1, HEAD_DIM), 1)
        half_dim = HEAD_DIM // 2
        index = jnp.where(lane < half_dim, lane, lane - half_dim).astype(f32)
        inverse_freq = 10000.0 ** (-2.0 * index / HEAD_DIM)
        angles = position * inverse_freq
        cos_ref[...] = jnp.cos(angles)
        sine = jnp.sin(angles)
        sin_ref[...] = jnp.where(lane < half_dim, -sine, sine)

    step_rows = 48 if rows % 48 == 0 else rows

    def update_k(i, carry):
        at = pl.ds(pl.multiple_of(i * step_rows, step_rows), step_rows)
        new = adamw(k_ref[0, at], k_ref[1, at], k_ref[2, at], k_ref[3, at])
        nmk[0, at], nek[0, at], nsk[0, at] = new
        gathered[0, dp, at] = new[0].astype(bf16)
        return carry

    def update_q(head):
        columns = slice(head * HEAD_DIM, (head + 1) * HEAD_DIM)

        def step(i, carry):
            at = pl.ds(pl.multiple_of(i * step_rows, step_rows), step_rows)
            new = adamw(*[q_ref[n, at, columns] for n in range(4)])
            nmq[0, at, columns], neq[0, at, columns], nsq[0, at, columns] = new
            gathered[1 + head, dp, at] = new[0].astype(bf16)
            return carry

        lax.fori_loop(0, rows // step_rows, step, 0)

    part_a = pl.ds(0, half_rows)
    part_b = pl.ds(half_rows, half_rows)

    def copy_to(peer, ref, piece, kind):
        return pltpu.make_async_remote_copy(
            src_ref=ref,
            dst_ref=ref,
            send_sem=send_sem.at[0],
            recv_sem=recv_sem.at[piece, kind],
            device_id=(peer, pipe, tensor),
            device_id_type=MESH,
        )

    def direct_copies(piece):
        own = gathered.at[piece, dp]
        peers = [3 - dp, x_side, y_side] if relayed else near
        return [copy_to(peer, own, piece, 2) for peer in peers]

    def own_copies(piece, kinds=range(4)):
        peers = (x_side, y_side, x_side, y_side)
        parts = (part_a, part_b, part_b, part_a)
        return [
            copy_to(peers[n], gathered.at[piece, dp, parts[n]], piece, min(n, 2))
            for n in kinds
        ]

    def relay_copies(piece):
        return [
            copy_to(y_side, gathered.at[piece, x_side, part_a], piece, 2),
            copy_to(x_side, gathered.at[piece, y_side, part_b], piece, 2),
        ]

    def send(piece, direct):
        for copy in direct_copies(piece) if direct or not relayed else own_copies(piece):
            copy.start()

    def relay(piece):
        if not relayed:
            return
        for got, passed in zip(own_copies(piece, (0, 1)), relay_copies(piece)):
            got.wait_recv()
            passed.start()

    def arrived(piece, direct):
        rest = n_dp - 1 if direct or not relayed else n_dp - 2
        copy_to(x_side, gathered.at[piece, pl.ds(0, rest)], piece, 2).wait_recv()

    def all_sent(count):
        whole = gathered.at[pl.ds(0, count), pl.ds(0, n_dp - 1)]
        copy_to(x_side, whole, 0, 2).wait_send()

    def weights(piece):
        return gathered[piece].reshape(n_dp * rows, HEAD_DIM)

    def rope(values, cosine, sine):
        return values * cosine + pltpu.roll(values, HEAD_DIM // 2, 1) * sine

    def key_or_value(values, is_key):
        cosine = jnp.where(is_key, cos_ref[...], 1.0)
        sine = jnp.where(is_key, sin_ref[...], 0.0)
        return rope(values, cosine, sine).astype(bf16)

    def project(head):
        queries = jnp.dot(normed_ref[...], weights(1 + head), preferred_element_type=f32)
        queries_ref[head] = rope(queries, cos_ref[...], sin_ref[...]).astype(bf16)

    def mix(queries):
        scores = lax.dot_general(
            queries, kv_ref[0], (((1,), (1,)), ((), ())), preferred_element_type=f32
        ) * HEAD_DIM ** (-0.5)
        scores = scores.reshape(-1, tokens, tokens)
        scores = jnp.where(mask_ref[...][None] > 0.5, scores, -1e30)
        row_max = jnp.max(scores, axis=2, keepdims=True)
        terms = jnp.exp(scores - row_max)
        probs = (terms / jnp.sum(terms, axis=2, keepdims=True)).astype(bf16)
        return jnp.dot(
            probs.reshape(-1, tokens), kv_ref[1], preferred_element_type=f32
        )

    def attend(head, residual):
        return (residual.astype(f32) + mix(queries_ref[head])).astype(bf16)

    def pair_block(source, target):
        return pltpu.make_async_remote_copy(
            src_ref=source,
            dst_ref=target,
            send_sem=pair_sem.at[0],
            recv_sem=pair_sem.at[1],
            device_id=(dp, pipe, pair),
            device_id_type=MESH,
        )

    def stream_copy(head, to_tensor):
        return pltpu.make_async_remote_copy(
            src_ref=first_ref.at[head],
            dst_ref=stream_ref.at[tensor * heads + head],
            send_sem=send_sem.at[1],
            recv_sem=stream_recv.at[tensor],
            device_id=(dp, 1, to_tensor),
            device_id_type=MESH,
        )

    def stream_group(blocks, source):
        return pltpu.make_async_remote_copy(
            src_ref=blocks,
            dst_ref=blocks,
            send_sem=send_sem.at[1],
            recv_sem=stream_recv.at[source],
            device_id=(dp, 1 - pipe, tensor),
            device_id_type=MESH,
        )

    weight_exchange = pair_block(gathered.at[0, dp], gathered.at[n_pieces, dp])

    pltpu.make_async_copy(k_ref, k_ref, load_sem.at[0]).wait()
    lax.fori_loop(0, rows // step_rows, update_k, 0)
    pl.semaphore_wait(barrier, len(near) + 1 + n_tensor - (n_tensor == 4))

    direct_pieces = (0, n_pieces - 1)

    @pl.when(pipe == 0)
    def _():
        send(0, True)

    @pl.when(pipe == 1)
    def _():
        weight_exchange.start()

    pltpu.make_async_copy(q_ref, q_ref, load_sem.at[1]).wait()
    for head in range(heads):
        update_q(head)

        @pl.when(pipe == 0)
        def _():
            send(1 + head, 1 + head in direct_pieces)

    load_x.wait()
    load_seg.wait()

    @pl.when(pipe == 0)
    def _():
        norm(lambda b: x_ref[:, b * HEAD_DIM : (b + 1) * HEAD_DIM].astype(f32))
        tables()
        exchange = pair_block(kv_ref.at[slot], kv_ref.at[slot])
        arrived(0, True)
        block = jnp.dot(normed_ref[...], weights(0), preferred_element_type=f32)
        kv_ref[slot] = key_or_value(block, holds_key)
        exchange.start()
        for p in range(1, n_pieces):
            if p not in direct_pieces:
                relay(p)
        pl.semaphore_signal(
            go_sem, inc=1, device_id=(dp, 1, tensor), device_id_type=MESH
        )
        for n in range(heads):
            head = (n + heads - 1) % heads
            arrived(1 + head, 1 + head in direct_pieces)
            project(head)
            if n == 0:
                exchange.wait()
            columns = pl.ds(
                pl.multiple_of((tensor * heads + head) * HEAD_DIM, HEAD_DIM), HEAD_DIM
            )
            result = attend(head, x_ref[:, columns])
            first_ref[head] = result
            for t in far_first:
                stream_copy(head, t).start()
            out_ref[:, head * HEAD_DIM : (head + 1) * HEAD_DIM] = result
        all_sent(n_pieces)
        stream_group(stream_ref, 0).wait_send()

    @pl.when(pipe == 1)
    def _():
        tables()
        weight_exchange.wait()
        order = [0, n_pieces] + list(range(1, n_pieces))
        pl.semaphore_wait(go_sem, 1)
        for p in order:
            send(p, False)
        for p in order:
            relay(p)
        for p in order[:-1] if blockwise else order:
            arrived(p, False)

        def stream_arrived(source):
            blocks = stream_ref.at[pl.ds(source * heads, heads)]
            stream_group(blocks, source).wait_recv()

        if blockwise:
            sources = far_first[::-1]
            split = (n_pieces) * HEAD_DIM

            def source_block(source):
                return jnp.concatenate(
                    [stream_ref[source * heads + h] for h in range(heads)], axis=1
                )

            def product(source, pieces):
                return jnp.dot(
                    source_block(source),
                    jnp.concatenate([gathered[p, source] for p in pieces], axis=1),
                    preferred_element_type=f32,
                )

            def add_squares(source, squares):
                for h in range(heads):
                    value = stream_ref[source * heads + h].astype(f32)
                    squares += value * value
                return squares

            squares = jnp.zeros((tokens, HEAD_DIM), f32)
            for n, source in enumerate(sources[:-1]):
                stream_arrived(source)
                squares = add_squares(source, squares)
                block = product(source, order[:-1])
                if n == 0:
                    sums_ref[:, :split] = block
                else:
                    sums_ref[:, :split] += block
            arrived(order[-1], False)
            block = product(sources[0], order[-1:])
            for source in sources[1:-1]:
                block += product(source, order[-1:])
            sums_ref[:, split:] = block
            stream_arrived(sources[-1])
            squares = add_squares(sources[-1], squares)
            sums_ref[...] += product(sources[-1], order)
            mean = jnp.sum(squares, axis=1, keepdims=True) / features
            scale = lax.rsqrt(mean + norm_eps)

            def projected(n):
                return sums_ref[:, n * HEAD_DIM : (n + 1) * HEAD_DIM] * scale

        else:
            for source in far_first:
                stream_arrived(source)
            norm(lambda b: stream_ref[b].astype(f32))

            def projected(n):
                return jnp.dot(
                    normed_ref[...], weights(order[n]), preferred_element_type=f32
                )

        kv_ref[slot] = key_or_value(projected(0), holds_key)
        kv_ref[1 - slot] = key_or_value(projected(1), jnp.logical_not(holds_key))
        queries = [
            rope(projected(2 + head), cos_ref[...], sin_ref[...]).astype(bf16)
            for head in range(heads)
        ]
        mixed = mix(jnp.concatenate(queries, axis=0))
        for head in range(heads):
            residual = stream_ref[tensor * heads + head].astype(f32)
            out_ref[:, head * HEAD_DIM : (head + 1) * HEAD_DIM] = (
                residual + mixed[head * tokens : (head + 1) * tokens]
            ).astype(bf16)
        all_sent(n_pieces + 1)


def sections_call(n_dp, n_tensor, stream, segments, q_arrays, kv_arrays):
    tokens, features = stream.shape
    _, rows, q_cols = q_arrays[0].shape
    kv_cols = kv_arrays[0].shape[2]
    heads = q_cols // HEAD_DIM
    n_pieces = 1 + heads
    bf16 = jnp.bfloat16
    f32 = jnp.float32
    vmem = pl.BlockSpec(memory_space=pltpu.VMEM)
    anywhere = pl.BlockSpec(memory_space=pl.ANY)
    return pl.pallas_call(
        functools.partial(sections_kernel, n_dp, n_tensor),
        out_shape=[pltpu.VMEM((1, rows, q_cols), f32)] * 3
        + [pltpu.VMEM((1, rows, kv_cols), f32)] * 3
        + [pltpu.VMEM((tokens, q_cols), bf16)],
        in_specs=[anywhere] * 10,
        out_specs=[vmem] * 7,
        scratch_shapes=[
            pltpu.VMEM((tokens, features), bf16),
            pltpu.VMEM(segments.shape, jnp.int32),
            pltpu.VMEM((4, rows, q_cols), f32),
            pltpu.VMEM((4, rows, kv_cols), f32),
            pltpu.SemaphoreType.DMA((4,)),
            pltpu.VMEM((n_pieces + 1, n_dp, rows, HEAD_DIM), bf16),
            pltpu.VMEM((tokens, features), bf16),
            pltpu.VMEM((tokens, HEAD_DIM), jnp.float32),
            pltpu.VMEM((tokens, HEAD_DIM), jnp.float32),
            pltpu.VMEM((tokens, tokens), jnp.float32),
            pltpu.VMEM((2, tokens, HEAD_DIM), bf16),
            pltpu.VMEM((heads, tokens, HEAD_DIM), bf16),
            pltpu.VMEM((tokens, (n_pieces + 1) * HEAD_DIM), f32),
            pltpu.VMEM((heads, tokens, HEAD_DIM), bf16),
            pltpu.VMEM((n_tensor * heads, tokens, HEAD_DIM), bf16),
            pltpu.SemaphoreType.DMA((2,)),
            pltpu.SemaphoreType.DMA((n_pieces + 1, 3)),
            pltpu.SemaphoreType.DMA((2,)),
            pltpu.SemaphoreType.DMA((n_tensor,)),
            pltpu.SemaphoreType.REGULAR,
        ],
        compiler_params=pltpu.CompilerParams(collective_id=0, has_side_effects=True),
    )(stream, segments, *q_arrays, *kv_arrays)


def solution(mesh):
    n_dp, n_tensor = mesh.shape["dp"], mesh.shape["tensor"]

    def on_device(
        stream_in,
        segment_ids,
        master_q,
        moment_q,
        second_q,
        grad_q,
        master_kv,
        moment_kv,
        second_kv,
        grad_kv,
    ):
        fresh = sections_call(
            n_dp,
            n_tensor,
            stream_in,
            segment_ids,
            (master_q, moment_q, second_q, grad_q),
            (master_kv, moment_kv, second_kv, grad_kv),
        )
        *states, result = write_call(fresh)
        return (*states, result[None])

    weight_spec = P("pipe", "dp", "tensor")
    return jax.shard_map(
        on_device,
        mesh=mesh,
        in_specs=(P("dp", None), P("dp", None)) + (weight_spec,) * 8,
        out_specs=(weight_spec,) * 7,
        check_vma=False,
    )
```

```python
import functools

import jax
import jax.numpy as jnp
from jax import lax
from jax.experimental import pallas as pl
from jax.experimental.pallas import tpu as pltpu
from jax.sharding import PartitionSpec as P

HEAD_DIM = 128
MESH = pl.DeviceIdType.MESH

beta_one = 0.9
beta_two = 0.999
adam_eps = 1e-08
learn_rate = 0.003
decay_rate = 0.1
adam_step = 10.0
norm_eps = 1e-05


def adamw(master, moment, second, gradient):
    moment_new = beta_one * moment + (1.0 - beta_one) * gradient
    second_new = beta_two * second + (1.0 - beta_two) * gradient * gradient
    fix_one = 1.0 - beta_one**adam_step
    fix_two = 1.0 - beta_two**adam_step
    step_dir = moment_new / fix_one / (jnp.sqrt(second_new / fix_two) + adam_eps)
    master_new = master - learn_rate * (step_dir + decay_rate * master)
    return (master_new, moment_new, second_new)


def write_kernel(*refs):
    count = (len(refs) - 1) // 2
    sems = refs[-1]
    copies = [
        pltpu.make_async_copy(refs[i], refs[count + i], sems.at[i]) for i in range(count)
    ]
    for copy in copies:
        copy.start()
    for copy in copies:
        copy.wait()


def write_call(arrays):
    return pl.pallas_call(
        write_kernel,
        in_specs=[pl.BlockSpec(memory_space=pltpu.VMEM)] * len(arrays),
        out_specs=[pl.BlockSpec(memory_space=pl.ANY)] * len(arrays),
        out_shape=[jax.ShapeDtypeStruct(a.shape, a.dtype) for a in arrays],
        scratch_shapes=[pltpu.SemaphoreType.DMA((len(arrays),))],
    )(*[pltpu.with_memory_space_constraint(a, pltpu.VMEM) for a in arrays])


def sections_kernel(
    n_dp,
    n_tensor,
    x_hbm,
    seg_hbm,
    mq_hbm,
    eq_hbm,
    sq_hbm,
    gq_hbm,
    mk_hbm,
    ek_hbm,
    sk_hbm,
    gk_hbm,
    nmq,
    neq,
    nsq,
    nmk,
    nek,
    nsk,
    out_ref,
    x_ref,
    seg_ref,
    q_ref,
    k_ref,
    load_sem,
    gathered,
    normed_ref,
    cos_ref,
    sin_ref,
    mask_ref,
    kv_ref,
    queries_ref,
    sums_ref,
    first_ref,
    stream_ref,
    lent_ref,
    send_sem,
    recv_sem,
    pair_sem,
    stream_recv,
    lent_sem,
    go_sem,
):
    dp = lax.axis_index("dp")
    pipe = lax.axis_index("pipe")
    tensor = lax.axis_index("tensor")
    tokens, features = x_ref.shape
    rows = q_ref.shape[1]
    heads = first_ref.shape[0]
    n_pieces = 1 + heads
    half_rows = rows // 2
    relayed = n_dp == 4
    half = n_tensor // 2
    pair = lax.rem(tensor + half, n_tensor)
    holds_key = tensor < half
    slot = jnp.where(holds_key, 0, 1)
    f32 = jnp.float32
    bf16 = jnp.bfloat16

    if n_tensor == 4:
        far_first = [3 - tensor, pair, tensor + 1 - 2 * lax.rem(tensor, 2), tensor]
    else:
        far_first = [lax.rem(tensor + off, n_tensor) for off in range(n_tensor)]
    lent = (2, 3) if n_dp == 4 and heads == 3 else ()
    blockwise = rows == heads * HEAD_DIM and n_dp == n_tensor

    x_side = dp + 1 - 2 * lax.rem(dp, 2)
    y_side = lax.rem(dp + 2, n_dp)

    barrier = pltpu.get_barrier_semaphore()
    if relayed:
        near = [x_side, y_side, 3 - dp]
    else:
        near = [lax.rem(dp + off, n_dp) for off in range(1, n_dp)]
    for peer in near:
        pl.semaphore_signal(
            barrier, inc=1, device_id=(peer, pipe, tensor), device_id_type=MESH
        )
    pl.semaphore_signal(barrier, inc=1, device_id=(dp, pipe, pair), device_id_type=MESH)
    for t in far_first[1:] if n_tensor == 4 else far_first:
        pl.semaphore_signal(
            barrier, inc=1, device_id=(dp, 1 - pipe, t), device_id_type=MESH
        )

    load_x = pltpu.make_async_copy(x_hbm, x_ref, load_sem.at[2])
    load_seg = pltpu.make_async_copy(seg_hbm, seg_ref, load_sem.at[3])
    for n, ref in enumerate((mk_hbm, ek_hbm, sk_hbm, gk_hbm)):
        pltpu.make_async_copy(ref.at[0], k_ref.at[n], load_sem.at[0]).start()
    for n, ref in enumerate((mq_hbm, eq_hbm, sq_hbm, gq_hbm)):
        pltpu.make_async_copy(ref.at[0], q_ref.at[n], load_sem.at[1]).start()
    load_x.start()
    load_seg.start()

    def norm(read_block):
        blocks = features // HEAD_DIM
        squares = jnp.zeros((tokens, HEAD_DIM), f32)
        for b in range(blocks):
            value = read_block(b)
            squares += value * value
        mean = jnp.sum(squares, axis=1, keepdims=True) / features
        scale = lax.rsqrt(mean + norm_eps)
        for b in range(blocks):
            normed_ref[:, b * HEAD_DIM : (b + 1) * HEAD_DIM] = (
                read_block(b) * scale
            ).astype(bf16)

    def tables():
        row = lax.broadcasted_iota(jnp.int32, (tokens, tokens), 0)
        col = lax.broadcasted_iota(jnp.int32, (tokens, tokens), 1)
        seg_row = jnp.broadcast_to(seg_ref[...].astype(f32), (tokens, tokens))
        seg_col = jnp.sum(jnp.where(row == col, seg_row, 0.0), axis=1, keepdims=True)
        same = seg_row == seg_col
        mask_ref[...] = jnp.where(same & (col <= row), 1.0, 0.0)
        position = jnp.sum(jnp.where(same & (col < row), 1.0, 0.0), axis=1, keepdims=True)
        lane = lax.broadcasted_iota(jnp.int32, (1, HEAD_DIM), 1)
        half_dim = HEAD_DIM // 2
        index = jnp.where(lane < half_dim, lane, lane - half_dim).astype(f32)
        inverse_freq = 10000.0 ** (-2.0 * index / HEAD_DIM)
        angles = position * inverse_freq
        cos_ref[...] = jnp.cos(angles)
        sine = jnp.sin(angles)
        sin_ref[...] = jnp.where(lane < half_dim, -sine, sine)

    step_rows = 48 if rows % 48 == 0 else rows

    def update_k(i, carry):
        at = pl.ds(pl.multiple_of(i * step_rows, step_rows), step_rows)
        new = adamw(k_ref[0, at], k_ref[1, at], k_ref[2, at], k_ref[3, at])
        nmk[0, at], nek[0, at], nsk[0, at] = new
        gathered[0, dp, at] = new[0].astype(bf16)
        return carry

    def update_q(head):
        columns = slice(head * HEAD_DIM, (head + 1) * HEAD_DIM)

        def step(i, carry):
            at = pl.ds(pl.multiple_of(i * step_rows, step_rows), step_rows)
            new = adamw(*[q_ref[n, at, columns] for n in range(4)])
            nmq[0, at, columns], neq[0, at, columns], nsq[0, at, columns] = new
            gathered[1 + head, dp, at] = new[0].astype(bf16)
            return carry

        lax.fori_loop(0, rows // step_rows, step, 0)

    part_a = pl.ds(0, half_rows)
    part_b = pl.ds(half_rows, half_rows)

    def copy_to(peer, ref, piece, kind, group=0):
        return pltpu.make_async_remote_copy(
            src_ref=ref,
            dst_ref=ref,
            send_sem=send_sem.at[group],
            recv_sem=recv_sem.at[piece, kind],
            device_id=(peer, pipe, tensor),
            device_id_type=MESH,
        )

    def direct_copies(piece):
        own = gathered.at[piece, dp]
        peers = [3 - dp, x_side, y_side] if relayed else near
        return [copy_to(peer, own, piece, 2) for peer in peers]

    def own_copies(piece, kinds=range(4)):
        peers = (x_side, y_side, x_side, y_side)
        parts = (part_a, part_b, part_b, part_a)
        return [
            copy_to(peers[n], gathered.at[piece, dp, parts[n]], piece, min(n, 2))
            for n in kinds
        ]

    def relay_copies(piece):
        group = 2 if piece in lent else 0
        return [
            copy_to(y_side, gathered.at[piece, x_side, part_a], piece, 2, group),
            copy_to(x_side, gathered.at[piece, y_side, part_b], piece, 2, group),
        ]

    def send(piece, direct):
        for copy in direct_copies(piece) if direct or not relayed else own_copies(piece):
            copy.start()

    def relay(piece):
        if not relayed:
            return
        for got, passed in zip(own_copies(piece, (0, 1)), relay_copies(piece)):
            got.wait_recv()
            passed.start()

    def arrived(piece, direct):
        rest = n_dp - 1 if direct or not relayed else n_dp - 2
        copy_to(x_side, gathered.at[piece, pl.ds(0, rest)], piece, 2).wait_recv()

    def all_sent(blocks, group):
        copy_to(x_side, blocks, 0, 2, group).wait_send()

    def weights(piece):
        return gathered[piece].reshape(n_dp * rows, HEAD_DIM)

    def rope(values, cosine, sine):
        return values * cosine + pltpu.roll(values, HEAD_DIM // 2, 1) * sine

    def key_or_value(values, is_key):
        cosine = jnp.where(is_key, cos_ref[...], 1.0)
        sine = jnp.where(is_key, sin_ref[...], 0.0)
        return rope(values, cosine, sine).astype(bf16)

    def project(head):
        queries = jnp.dot(normed_ref[...], weights(1 + head), preferred_element_type=f32)
        queries_ref[head] = rope(queries, cos_ref[...], sin_ref[...]).astype(bf16)

    def mix(queries):
        scores = lax.dot_general(
            queries, kv_ref[0], (((1,), (1,)), ((), ())), preferred_element_type=f32
        ) * HEAD_DIM ** (-0.5)
        scores = scores.reshape(-1, tokens, tokens)
        scores = jnp.where(mask_ref[...][None] > 0.5, scores, -1e30)
        row_max = jnp.max(scores, axis=2, keepdims=True)
        terms = jnp.exp(scores - row_max)
        probs = (terms / jnp.sum(terms, axis=2, keepdims=True)).astype(bf16)
        return jnp.dot(
            probs.reshape(-1, tokens), kv_ref[1], preferred_element_type=f32
        )

    def attend(head, residual):
        return (residual.astype(f32) + mix(queries_ref[head])).astype(bf16)

    def pair_block(source, target):
        return pltpu.make_async_remote_copy(
            src_ref=source,
            dst_ref=target,
            send_sem=pair_sem.at[0],
            recv_sem=pair_sem.at[1],
            device_id=(dp, pipe, pair),
            device_id_type=MESH,
        )

    def stream_copy(head, to_tensor):
        return pltpu.make_async_remote_copy(
            src_ref=first_ref.at[head],
            dst_ref=stream_ref.at[tensor * heads + head],
            send_sem=send_sem.at[1],
            recv_sem=stream_recv.at[tensor],
            device_id=(dp, 1, to_tensor),
            device_id_type=MESH,
        )

    def stream_group(blocks, source):
        return pltpu.make_async_remote_copy(
            src_ref=blocks,
            dst_ref=blocks,
            send_sem=send_sem.at[1],
            recv_sem=stream_recv.at[source],
            device_id=(dp, 1 - pipe, tensor),
            device_id_type=MESH,
        )

    def lend(piece):
        return pltpu.make_async_remote_copy(
            src_ref=gathered.at[piece, dp],
            dst_ref=lent_ref.at[lent.index(piece)],
            send_sem=lent_sem.at[0],
            recv_sem=lent_sem.at[1],
            device_id=(dp, 0, tensor),
            device_id_type=MESH,
        )

    def lent_group():
        return pltpu.make_async_remote_copy(
            src_ref=lent_ref,
            dst_ref=lent_ref,
            send_sem=lent_sem.at[0],
            recv_sem=lent_sem.at[1],
            device_id=(dp, 1 - pipe, tensor),
            device_id_type=MESH,
        )

    def send_lent(piece):
        peers = (x_side, y_side, x_side, y_side)
        parts = (part_a, part_b, part_b, part_a)
        for n in range(4):
            pltpu.make_async_remote_copy(
                src_ref=lent_ref.at[lent.index(piece), parts[n]],
                dst_ref=gathered.at[piece, dp, parts[n]],
                send_sem=send_sem.at[2],
                recv_sem=recv_sem.at[piece, min(n, 2)],
                device_id=(peers[n], 1, tensor),
                device_id_type=MESH,
            ).start()

    weight_exchange = pair_block(gathered.at[0, dp], gathered.at[n_pieces, dp])

    pltpu.make_async_copy(k_ref, k_ref, load_sem.at[0]).wait()
    lax.fori_loop(0, rows // step_rows, update_k, 0)
    pl.semaphore_wait(barrier, len(near) + 1 + n_tensor - (n_tensor == 4))

    @pl.when(pipe == 0)
    def _():
        send(0, True)

    @pl.when(pipe == 1)
    def _():
        weight_exchange.start()

    pltpu.make_async_copy(q_ref, q_ref, load_sem.at[1]).wait()
    for head in range(heads):
        update_q(head)

        @pl.when(pipe == 0)
        def _():
            send(1 + head, True)

        if 1 + head in lent:

            @pl.when(pipe == 1)
            def _():
                lend(1 + head).start()

    load_x.wait()
    load_seg.wait()

    @pl.when(pipe == 0)
    def _():
        norm(lambda b: x_ref[:, b * HEAD_DIM : (b + 1) * HEAD_DIM].astype(f32))
        tables()
        exchange = pair_block(kv_ref.at[slot], kv_ref.at[slot])
        if lent:
            lent_group().wait_recv()
            for p in lent:
                send_lent(p)
        arrived(0, True)
        block = jnp.dot(normed_ref[...], weights(0), preferred_element_type=f32)
        kv_ref[slot] = key_or_value(block, holds_key)
        exchange.start()
        for head in range(heads):
            arrived(1 + head, True)
            project(head)
            if head == 0:
                pl.semaphore_signal(
                    go_sem, inc=1, device_id=(dp, 1, tensor), device_id_type=MESH
                )
                exchange.wait()
            columns = pl.ds(
                pl.multiple_of((tensor * heads + head) * HEAD_DIM, HEAD_DIM), HEAD_DIM
            )
            result = attend(head, x_ref[:, columns])
            first_ref[head] = result
            for t in far_first:
                stream_copy(head, t).start()
            out_ref[:, head * HEAD_DIM : (head + 1) * HEAD_DIM] = result
        all_sent(gathered.at[pl.ds(0, n_pieces), pl.ds(0, n_dp - 1)], 0)
        if lent:
            all_sent(gathered.at[0], 2)
        stream_group(stream_ref, 0).wait_send()

    @pl.when(pipe == 1)
    def _():
        tables()
        weight_exchange.wait()
        order = [0, n_pieces] + list(range(1, n_pieces))
        if lent:
            order = [0, n_pieces, 2, 3, 1]
        pl.semaphore_wait(go_sem, 1)
        for p in order:
            if p not in lent:
                send(p, False)
        for p in [0, 2, n_pieces, 3, 1] if lent else order:
            relay(p)
        for p in order[:-1] if blockwise else order:
            arrived(p, False)

        def stream_arrived(source):
            blocks = stream_ref.at[pl.ds(source * heads, heads)]
            stream_group(blocks, source).wait_recv()

        if blockwise:
            sources = far_first[::-1]
            split = (n_pieces) * HEAD_DIM

            def source_block(source):
                return jnp.concatenate(
                    [stream_ref[source * heads + h] for h in range(heads)], axis=1
                )

            def product(source, pieces):
                return jnp.dot(
                    source_block(source),
                    jnp.concatenate([gathered[p, source] for p in pieces], axis=1),
                    preferred_element_type=f32,
                )

            def add_squares(source, squares):
                for h in range(heads):
                    value = stream_ref[source * heads + h].astype(f32)
                    squares += value * value
                return squares

            squares = jnp.zeros((tokens, HEAD_DIM), f32)
            for n, source in enumerate(sources[:-1]):
                stream_arrived(source)
                squares = add_squares(source, squares)
                block = product(source, order[:-1])
                if n == 0:
                    sums_ref[:, :split] = block
                else:
                    sums_ref[:, :split] += block
            arrived(order[-1], False)
            block = product(sources[0], order[-1:])
            for source in sources[1:-1]:
                block += product(source, order[-1:])
            sums_ref[:, split:] = block
            stream_arrived(sources[-1])
            squares = add_squares(sources[-1], squares)
            sums_ref[...] += product(sources[-1], order)
            mean = jnp.sum(squares, axis=1, keepdims=True) / features
            scale = lax.rsqrt(mean + norm_eps)

            def projected(n):
                return sums_ref[:, n * HEAD_DIM : (n + 1) * HEAD_DIM] * scale

        else:
            for source in far_first:
                stream_arrived(source)
            norm(lambda b: stream_ref[b].astype(f32))

            def projected(n):
                return jnp.dot(
                    normed_ref[...], weights(order[n]), preferred_element_type=f32
                )

        kv_ref[slot] = key_or_value(projected(0), holds_key)
        kv_ref[1 - slot] = key_or_value(projected(1), jnp.logical_not(holds_key))
        queries = [
            rope(projected(order.index(1 + head)), cos_ref[...], sin_ref[...]).astype(bf16)
            for head in range(heads)
        ]
        mixed = mix(jnp.concatenate(queries, axis=0))
        for head in range(heads):
            residual = stream_ref[tensor * heads + head].astype(f32)
            out_ref[:, head * HEAD_DIM : (head + 1) * HEAD_DIM] = (
                residual + mixed[head * tokens : (head + 1) * tokens]
            ).astype(bf16)
        rest = n_pieces + 1 - len(lent)
        all_sent(gathered.at[pl.ds(0, rest), pl.ds(0, n_dp - 1)], 0)
        if lent:
            all_sent(gathered.at[0, pl.ds(0, len(lent))], 2)
            lent_group().wait_send()


def sections_call(n_dp, n_tensor, stream, segments, q_arrays, kv_arrays):
    tokens, features = stream.shape
    _, rows, q_cols = q_arrays[0].shape
    kv_cols = kv_arrays[0].shape[2]
    heads = q_cols // HEAD_DIM
    n_pieces = 1 + heads
    bf16 = jnp.bfloat16
    f32 = jnp.float32
    vmem = pl.BlockSpec(memory_space=pltpu.VMEM)
    anywhere = pl.BlockSpec(memory_space=pl.ANY)
    return pl.pallas_call(
        functools.partial(sections_kernel, n_dp, n_tensor),
        out_shape=[pltpu.VMEM((1, rows, q_cols), f32)] * 3
        + [pltpu.VMEM((1, rows, kv_cols), f32)] * 3
        + [pltpu.VMEM((tokens, q_cols), bf16)],
        in_specs=[anywhere] * 10,
        out_specs=[vmem] * 7,
        scratch_shapes=[
            pltpu.VMEM((tokens, features), bf16),
            pltpu.VMEM(segments.shape, jnp.int32),
            pltpu.VMEM((4, rows, q_cols), f32),
            pltpu.VMEM((4, rows, kv_cols), f32),
            pltpu.SemaphoreType.DMA((4,)),
            pltpu.VMEM((n_pieces + 1, n_dp, rows, HEAD_DIM), bf16),
            pltpu.VMEM((tokens, features), bf16),
            pltpu.VMEM((tokens, HEAD_DIM), jnp.float32),
            pltpu.VMEM((tokens, HEAD_DIM), jnp.float32),
            pltpu.VMEM((tokens, tokens), jnp.float32),
            pltpu.VMEM((2, tokens, HEAD_DIM), bf16),
            pltpu.VMEM((heads, tokens, HEAD_DIM), bf16),
            pltpu.VMEM((tokens, (n_pieces + 1) * HEAD_DIM), f32),
            pltpu.VMEM((heads, tokens, HEAD_DIM), bf16),
            pltpu.VMEM((n_tensor * heads, tokens, HEAD_DIM), bf16),
            pltpu.VMEM((2, rows, HEAD_DIM), bf16),
            pltpu.SemaphoreType.DMA((3,)),
            pltpu.SemaphoreType.DMA((n_pieces + 1, 3)),
            pltpu.SemaphoreType.DMA((2,)),
            pltpu.SemaphoreType.DMA((n_tensor,)),
            pltpu.SemaphoreType.DMA((2,)),
            pltpu.SemaphoreType.REGULAR,
        ],
        compiler_params=pltpu.CompilerParams(collective_id=0, has_side_effects=True),
    )(stream, segments, *q_arrays, *kv_arrays)


def solution(mesh):
    n_dp, n_tensor = mesh.shape["dp"], mesh.shape["tensor"]

    def on_device(
        stream_in,
        segment_ids,
        master_q,
        moment_q,
        second_q,
        grad_q,
        master_kv,
        moment_kv,
        second_kv,
        grad_kv,
    ):
        fresh = sections_call(
            n_dp,
            n_tensor,
            stream_in,
            segment_ids,
            (master_q, moment_q, second_q, grad_q),
            (master_kv, moment_kv, second_kv, grad_kv),
        )
        *states, result = write_call(fresh)
        return (*states, result[None])

    weight_spec = P("pipe", "dp", "tensor")
    return jax.shard_map(
        on_device,
        mesh=mesh,
        in_specs=(P("dp", None), P("dp", None)) + (weight_spec,) * 8,
        out_specs=(weight_spec,) * 7,
        check_vma=False,
    )
```

```python
import functools

import jax
import jax.numpy as jnp
from jax import lax
from jax.experimental import pallas as pl
from jax.experimental.pallas import tpu as pltpu
from jax.sharding import PartitionSpec as P

HEAD_DIM = 128
MESH = pl.DeviceIdType.MESH

beta_one = 0.9
beta_two = 0.999
adam_eps = 1e-08
learn_rate = 0.003
decay_rate = 0.1
adam_step = 10.0
norm_eps = 1e-05


def adamw(master, moment, second, gradient):
    moment_new = beta_one * moment + (1.0 - beta_one) * gradient
    second_new = beta_two * second + (1.0 - beta_two) * gradient * gradient
    fix_one = 1.0 - beta_one**adam_step
    fix_two = 1.0 - beta_two**adam_step
    step_dir = moment_new / fix_one / (jnp.sqrt(second_new / fix_two) + adam_eps)
    master_new = master - learn_rate * (step_dir + decay_rate * master)
    return (master_new, moment_new, second_new)


def write_kernel(*refs):
    count = (len(refs) - 1) // 2
    sems = refs[-1]
    copies = [
        pltpu.make_async_copy(refs[i], refs[count + i], sems.at[i]) for i in range(count)
    ]
    for copy in copies:
        copy.start()
    for copy in copies:
        copy.wait()


def write_call(arrays):
    return pl.pallas_call(
        write_kernel,
        in_specs=[pl.BlockSpec(memory_space=pltpu.VMEM)] * len(arrays),
        out_specs=[pl.BlockSpec(memory_space=pl.ANY)] * len(arrays),
        out_shape=[jax.ShapeDtypeStruct(a.shape, a.dtype) for a in arrays],
        scratch_shapes=[pltpu.SemaphoreType.DMA((len(arrays),))],
    )(*[pltpu.with_memory_space_constraint(a, pltpu.VMEM) for a in arrays])


def sections_kernel(
    n_dp,
    n_tensor,
    x_hbm,
    seg_hbm,
    mq_hbm,
    eq_hbm,
    sq_hbm,
    gq_hbm,
    mk_hbm,
    ek_hbm,
    sk_hbm,
    gk_hbm,
    nmq,
    neq,
    nsq,
    nmk,
    nek,
    nsk,
    out_ref,
    x_ref,
    seg_ref,
    q_ref,
    k_ref,
    load_sem,
    gathered,
    normed_ref,
    cos_ref,
    sin_ref,
    mask_ref,
    kv_ref,
    queries_ref,
    sums_ref,
    first_ref,
    stream_ref,
    lent_ref,
    send_sem,
    recv_sem,
    pair_sem,
    stream_recv,
    lent_sem,
    go_sem,
):
    dp = lax.axis_index("dp")
    pipe = lax.axis_index("pipe")
    tensor = lax.axis_index("tensor")
    tokens, features = x_ref.shape
    rows = q_ref.shape[1]
    heads = first_ref.shape[0]
    n_pieces = 1 + heads
    half_rows = rows // 2
    relayed = n_dp == 4
    half = n_tensor // 2
    pair = lax.rem(tensor + half, n_tensor)
    holds_key = tensor < half
    slot = jnp.where(holds_key, 0, 1)
    f32 = jnp.float32
    bf16 = jnp.bfloat16

    if n_tensor == 4:
        far_first = [3 - tensor, pair, tensor + 1 - 2 * lax.rem(tensor, 2), tensor]
    else:
        far_first = [lax.rem(tensor + off, n_tensor) for off in range(n_tensor)]
    lent = (2, 3) if n_dp == 4 and heads == 3 else ()
    blockwise = rows == heads * HEAD_DIM and n_dp == n_tensor

    x_side = dp + 1 - 2 * lax.rem(dp, 2)
    y_side = lax.rem(dp + 2, n_dp)

    barrier = pltpu.get_barrier_semaphore()
    if relayed:
        near = [x_side, y_side, 3 - dp]
    else:
        near = [lax.rem(dp + off, n_dp) for off in range(1, n_dp)]
    for peer in near:
        pl.semaphore_signal(
            barrier, inc=1, device_id=(peer, pipe, tensor), device_id_type=MESH
        )
    pl.semaphore_signal(barrier, inc=1, device_id=(dp, pipe, pair), device_id_type=MESH)
    for t in far_first[1:] if n_tensor == 4 else far_first:
        pl.semaphore_signal(
            barrier, inc=1, device_id=(dp, 1 - pipe, t), device_id_type=MESH
        )

    load_x = pltpu.make_async_copy(x_hbm, x_ref, load_sem.at[2])
    load_seg = pltpu.make_async_copy(seg_hbm, seg_ref, load_sem.at[3])
    for n, ref in enumerate((mk_hbm, ek_hbm, sk_hbm, gk_hbm)):
        pltpu.make_async_copy(ref.at[0], k_ref.at[n], load_sem.at[0]).start()
    for n, ref in enumerate((mq_hbm, eq_hbm, sq_hbm, gq_hbm)):
        pltpu.make_async_copy(ref.at[0], q_ref.at[n], load_sem.at[1]).start()
    load_x.start()
    load_seg.start()

    def norm(read_block):
        blocks = features // HEAD_DIM
        squares = jnp.zeros((tokens, HEAD_DIM), f32)
        for b in range(blocks):
            value = read_block(b)
            squares += value * value
        mean = jnp.sum(squares, axis=1, keepdims=True) / features
        scale = lax.rsqrt(mean + norm_eps)
        for b in range(blocks):
            normed_ref[:, b * HEAD_DIM : (b + 1) * HEAD_DIM] = (
                read_block(b) * scale
            ).astype(bf16)

    def tables():
        row = lax.broadcasted_iota(jnp.int32, (tokens, tokens), 0)
        col = lax.broadcasted_iota(jnp.int32, (tokens, tokens), 1)
        seg_row = jnp.broadcast_to(seg_ref[...].astype(f32), (tokens, tokens))
        seg_col = jnp.sum(jnp.where(row == col, seg_row, 0.0), axis=1, keepdims=True)
        same = seg_row == seg_col
        mask_ref[...] = jnp.where(same & (col <= row), 1.0, 0.0)
        position = jnp.sum(jnp.where(same & (col < row), 1.0, 0.0), axis=1, keepdims=True)
        lane = lax.broadcasted_iota(jnp.int32, (1, HEAD_DIM), 1)
        half_dim = HEAD_DIM // 2
        index = jnp.where(lane < half_dim, lane, lane - half_dim).astype(f32)
        inverse_freq = 10000.0 ** (-2.0 * index / HEAD_DIM)
        angles = position * inverse_freq
        cos_ref[...] = jnp.cos(angles)
        sine = jnp.sin(angles)
        sin_ref[...] = jnp.where(lane < half_dim, -sine, sine)

    step_rows = 48 if rows % 48 == 0 else rows

    def update_k(i, carry):
        at = pl.ds(pl.multiple_of(i * step_rows, step_rows), step_rows)
        new = adamw(k_ref[0, at], k_ref[1, at], k_ref[2, at], k_ref[3, at])
        nmk[0, at], nek[0, at], nsk[0, at] = new
        gathered[0, dp, at] = new[0].astype(bf16)
        return carry

    def update_q(head):
        columns = slice(head * HEAD_DIM, (head + 1) * HEAD_DIM)

        def step(i, carry):
            at = pl.ds(pl.multiple_of(i * step_rows, step_rows), step_rows)
            new = adamw(*[q_ref[n, at, columns] for n in range(4)])
            nmq[0, at, columns], neq[0, at, columns], nsq[0, at, columns] = new
            gathered[1 + head, dp, at] = new[0].astype(bf16)
            return carry

        lax.fori_loop(0, rows // step_rows, step, 0)

    part_a = pl.ds(0, half_rows)
    part_b = pl.ds(half_rows, half_rows)

    def copy_to(peer, ref, piece, kind, group=0):
        return pltpu.make_async_remote_copy(
            src_ref=ref,
            dst_ref=ref,
            send_sem=send_sem.at[group],
            recv_sem=recv_sem.at[piece, kind],
            device_id=(peer, pipe, tensor),
            device_id_type=MESH,
        )

    def direct_copies(piece):
        own = gathered.at[piece, dp]
        peers = [3 - dp, x_side, y_side] if relayed else near
        return [copy_to(peer, own, piece, 2) for peer in peers]

    def own_copies(piece, kinds=range(4)):
        peers = (x_side, y_side, x_side, y_side)
        parts = (part_a, part_b, part_b, part_a)
        return [
            copy_to(peers[n], gathered.at[piece, dp, parts[n]], piece, min(n, 2))
            for n in kinds
        ]

    def relay_copies(piece):
        group = 2 if piece in lent else 0
        return [
            copy_to(y_side, gathered.at[piece, x_side, part_a], piece, 2, group),
            copy_to(x_side, gathered.at[piece, y_side, part_b], piece, 2, group),
        ]

    def send(piece, direct):
        for copy in direct_copies(piece) if direct or not relayed else own_copies(piece):
            copy.start()

    def relay(piece):
        if not relayed:
            return
        for got, passed in zip(own_copies(piece, (0, 1)), relay_copies(piece)):
            got.wait_recv()
            passed.start()

    def arrived(piece, direct):
        rest = n_dp - 1 if direct or not relayed else n_dp - 2
        copy_to(x_side, gathered.at[piece, pl.ds(0, rest)], piece, 2).wait_recv()

    def all_sent(blocks, group):
        copy_to(x_side, blocks, 0, 2, group).wait_send()

    def weights(piece):
        return gathered[piece].reshape(n_dp * rows, HEAD_DIM)

    def rope(values, cosine, sine):
        return values * cosine + pltpu.roll(values, HEAD_DIM // 2, 1) * sine

    def key_or_value(values, is_key):
        cosine = jnp.where(is_key, cos_ref[...], 1.0)
        sine = jnp.where(is_key, sin_ref[...], 0.0)
        return rope(values, cosine, sine).astype(bf16)

    def project(head):
        queries = jnp.dot(normed_ref[...], weights(1 + head), preferred_element_type=f32)
        queries_ref[head] = rope(queries, cos_ref[...], sin_ref[...]).astype(bf16)

    def mix(queries):
        scores = lax.dot_general(
            queries, kv_ref[0], (((1,), (1,)), ((), ())), preferred_element_type=f32
        ) * HEAD_DIM ** (-0.5)
        scores = scores.reshape(-1, tokens, tokens)
        scores = jnp.where(mask_ref[...][None] > 0.5, scores, -1e30)
        row_max = jnp.max(scores, axis=2, keepdims=True)
        terms = jnp.exp(scores - row_max)
        probs = (terms / jnp.sum(terms, axis=2, keepdims=True)).astype(bf16)
        return jnp.dot(
            probs.reshape(-1, tokens), kv_ref[1], preferred_element_type=f32
        )

    def attend(head, residual):
        return (residual.astype(f32) + mix(queries_ref[head])).astype(bf16)

    def pair_block(source, target):
        return pltpu.make_async_remote_copy(
            src_ref=source,
            dst_ref=target,
            send_sem=pair_sem.at[0],
            recv_sem=pair_sem.at[1],
            device_id=(dp, pipe, pair),
            device_id_type=MESH,
        )

    def stream_copy(head, to_tensor):
        return pltpu.make_async_remote_copy(
            src_ref=first_ref.at[head],
            dst_ref=stream_ref.at[tensor * heads + head],
            send_sem=send_sem.at[1],
            recv_sem=stream_recv.at[tensor],
            device_id=(dp, 1, to_tensor),
            device_id_type=MESH,
        )

    def stream_group(blocks, source):
        return pltpu.make_async_remote_copy(
            src_ref=blocks,
            dst_ref=blocks,
            send_sem=send_sem.at[1],
            recv_sem=stream_recv.at[source],
            device_id=(dp, 1 - pipe, tensor),
            device_id_type=MESH,
        )

    def lend(piece):
        return pltpu.make_async_remote_copy(
            src_ref=gathered.at[piece, dp],
            dst_ref=lent_ref.at[lent.index(piece)],
            send_sem=lent_sem.at[0],
            recv_sem=lent_sem.at[1],
            device_id=(dp, 1 - pipe, tensor),
            device_id_type=MESH,
        )

    def lent_group():
        return pltpu.make_async_remote_copy(
            src_ref=lent_ref,
            dst_ref=lent_ref,
            send_sem=lent_sem.at[0],
            recv_sem=lent_sem.at[1],
            device_id=(dp, 1 - pipe, tensor),
            device_id_type=MESH,
        )

    def send_lent(piece):
        peers = (x_side, y_side, x_side, y_side)
        parts = (part_a, part_b, part_b, part_a)
        for n in range(4):
            pltpu.make_async_remote_copy(
                src_ref=lent_ref.at[lent.index(piece), parts[n]],
                dst_ref=gathered.at[piece, dp, parts[n]],
                send_sem=send_sem.at[2],
                recv_sem=recv_sem.at[piece, min(n, 2)],
                device_id=(peers[n], 1, tensor),
                device_id_type=MESH,
            ).start()

    def send_lent_direct(piece):
        for peer in (3 - dp, x_side, y_side):
            pltpu.make_async_remote_copy(
                src_ref=lent_ref.at[lent.index(piece)],
                dst_ref=gathered.at[piece, dp],
                send_sem=send_sem.at[1],
                recv_sem=recv_sem.at[piece, 2],
                device_id=(peer, 0, tensor),
                device_id_type=MESH,
            ).start()

    weight_exchange = pair_block(gathered.at[0, dp], gathered.at[n_pieces, dp])

    pltpu.make_async_copy(k_ref, k_ref, load_sem.at[0]).wait()
    lax.fori_loop(0, rows // step_rows, update_k, 0)
    pl.semaphore_wait(barrier, len(near) + 1 + n_tensor - (n_tensor == 4))

    @pl.when(pipe == 0)
    def _():
        send(0, True)

    @pl.when(pipe == 1)
    def _():
        weight_exchange.start()

    pltpu.make_async_copy(q_ref, q_ref, load_sem.at[1]).wait()
    for head in range(heads):
        update_q(head)

        if 1 + head in lent:
            lend(1 + head).start()
        else:

            @pl.when(pipe == 0)
            def _():
                send(1 + head, True)

    load_x.wait()
    load_seg.wait()

    @pl.when(pipe == 0)
    def _():
        norm(lambda b: x_ref[:, b * HEAD_DIM : (b + 1) * HEAD_DIM].astype(f32))
        tables()
        exchange = pair_block(kv_ref.at[slot], kv_ref.at[slot])
        if lent:
            lent_group().wait_recv()
            for p in lent:
                send_lent(p)
        arrived(0, True)
        block = jnp.dot(normed_ref[...], weights(0), preferred_element_type=f32)
        kv_ref[slot] = key_or_value(block, holds_key)
        exchange.start()
        for head in range(heads):
            arrived(1 + head, True)
            project(head)
            if head == 0:
                if not lent:
                    pl.semaphore_signal(
                        go_sem, inc=1, device_id=(dp, 1, tensor), device_id_type=MESH
                    )
                exchange.wait()
            columns = pl.ds(
                pl.multiple_of((tensor * heads + head) * HEAD_DIM, HEAD_DIM), HEAD_DIM
            )
            result = attend(head, x_ref[:, columns])
            first_ref[head] = result
            for t in far_first:
                stream_copy(head, t).start()
            out_ref[:, head * HEAD_DIM : (head + 1) * HEAD_DIM] = result
        all_sent(gathered.at[pl.ds(0, n_pieces - len(lent)), pl.ds(0, n_dp - 1)], 0)
        if lent:
            all_sent(gathered.at[0], 2)
            lent_group().wait_send()
        stream_group(stream_ref, 0).wait_send()

    @pl.when(pipe == 1)
    def _():
        if lent:
            lent_group().wait_recv()
            for p in lent:
                send_lent_direct(p)
        else:
            pl.semaphore_wait(go_sem, 1)
        weight_exchange.wait()
        order = [0, n_pieces] + list(range(1, n_pieces))
        if lent:
            order = [0, n_pieces, 2, 3, 1]
        for p in order:
            if p not in lent:
                send(p, False)
        tables()
        for p in [2, 0, 3, n_pieces, 1] if lent else order:
            relay(p)
        for p in order[:-1] if blockwise else order:
            arrived(p, False)

        def stream_arrived(source):
            blocks = stream_ref.at[pl.ds(source * heads, heads)]
            stream_group(blocks, source).wait_recv()

        if blockwise:
            sources = far_first[::-1]
            split = (n_pieces) * HEAD_DIM

            def source_block(source):
                return jnp.concatenate(
                    [stream_ref[source * heads + h] for h in range(heads)], axis=1
                )

            def product(source, pieces):
                return jnp.dot(
                    source_block(source),
                    jnp.concatenate([gathered[p, source] for p in pieces], axis=1),
                    preferred_element_type=f32,
                )

            def add_squares(source, squares):
                for h in range(heads):
                    value = stream_ref[source * heads + h].astype(f32)
                    squares += value * value
                return squares

            squares = jnp.zeros((tokens, HEAD_DIM), f32)
            for n, source in enumerate(sources[:-1]):
                stream_arrived(source)
                squares = add_squares(source, squares)
                block = product(source, order[:-1])
                if n == 0:
                    sums_ref[:, :split] = block
                else:
                    sums_ref[:, :split] += block
            arrived(order[-1], False)
            block = product(sources[0], order[-1:])
            for source in sources[1:-1]:
                block += product(source, order[-1:])
            sums_ref[:, split:] = block
            stream_arrived(sources[-1])
            squares = add_squares(sources[-1], squares)
            sums_ref[...] += product(sources[-1], order)
            mean = jnp.sum(squares, axis=1, keepdims=True) / features
            scale = lax.rsqrt(mean + norm_eps)

            def projected(n):
                return sums_ref[:, n * HEAD_DIM : (n + 1) * HEAD_DIM] * scale

        else:
            for source in far_first:
                stream_arrived(source)
            norm(lambda b: stream_ref[b].astype(f32))

            def projected(n):
                return jnp.dot(
                    normed_ref[...], weights(order[n]), preferred_element_type=f32
                )

        kv_ref[slot] = key_or_value(projected(0), holds_key)
        kv_ref[1 - slot] = key_or_value(projected(1), jnp.logical_not(holds_key))
        queries = [
            rope(projected(order.index(1 + head)), cos_ref[...], sin_ref[...]).astype(bf16)
            for head in range(heads)
        ]
        mixed = mix(jnp.concatenate(queries, axis=0))
        for head in range(heads):
            residual = stream_ref[tensor * heads + head].astype(f32)
            out_ref[:, head * HEAD_DIM : (head + 1) * HEAD_DIM] = (
                residual + mixed[head * tokens : (head + 1) * tokens]
            ).astype(bf16)
        rest = n_pieces + 1 - len(lent)
        all_sent(gathered.at[pl.ds(0, rest), pl.ds(0, n_dp - 1)], 0)
        if lent:
            all_sent(gathered.at[0, pl.ds(0, len(lent))], 2)
            all_sent(gathered.at[pl.ds(0, len(lent)), pl.ds(0, n_dp - 1)], 1)
            lent_group().wait_send()


def sections_call(n_dp, n_tensor, stream, segments, q_arrays, kv_arrays):
    tokens, features = stream.shape
    _, rows, q_cols = q_arrays[0].shape
    kv_cols = kv_arrays[0].shape[2]
    heads = q_cols // HEAD_DIM
    n_pieces = 1 + heads
    bf16 = jnp.bfloat16
    f32 = jnp.float32
    vmem = pl.BlockSpec(memory_space=pltpu.VMEM)
    anywhere = pl.BlockSpec(memory_space=pl.ANY)
    return pl.pallas_call(
        functools.partial(sections_kernel, n_dp, n_tensor),
        out_shape=[pltpu.VMEM((1, rows, q_cols), f32)] * 3
        + [pltpu.VMEM((1, rows, kv_cols), f32)] * 3
        + [pltpu.VMEM((tokens, q_cols), bf16)],
        in_specs=[anywhere] * 10,
        out_specs=[vmem] * 7,
        scratch_shapes=[
            pltpu.VMEM((tokens, features), bf16),
            pltpu.VMEM(segments.shape, jnp.int32),
            pltpu.VMEM((4, rows, q_cols), f32),
            pltpu.VMEM((4, rows, kv_cols), f32),
            pltpu.SemaphoreType.DMA((4,)),
            pltpu.VMEM((n_pieces + 1, n_dp, rows, HEAD_DIM), bf16),
            pltpu.VMEM((tokens, features), bf16),
            pltpu.VMEM((tokens, HEAD_DIM), jnp.float32),
            pltpu.VMEM((tokens, HEAD_DIM), jnp.float32),
            pltpu.VMEM((tokens, tokens), jnp.float32),
            pltpu.VMEM((2, tokens, HEAD_DIM), bf16),
            pltpu.VMEM((heads, tokens, HEAD_DIM), bf16),
            pltpu.VMEM((tokens, (n_pieces + 1) * HEAD_DIM), f32),
            pltpu.VMEM((heads, tokens, HEAD_DIM), bf16),
            pltpu.VMEM((n_tensor * heads, tokens, HEAD_DIM), bf16),
            pltpu.VMEM((2, rows, HEAD_DIM), bf16),
            pltpu.SemaphoreType.DMA((3,)),
            pltpu.SemaphoreType.DMA((n_pieces + 1, 3)),
            pltpu.SemaphoreType.DMA((2,)),
            pltpu.SemaphoreType.DMA((n_tensor,)),
            pltpu.SemaphoreType.DMA((2,)),
            pltpu.SemaphoreType.REGULAR,
        ],
        compiler_params=pltpu.CompilerParams(collective_id=0, has_side_effects=True),
    )(stream, segments, *q_arrays, *kv_arrays)


def solution(mesh):
    n_dp, n_tensor = mesh.shape["dp"], mesh.shape["tensor"]

    def on_device(
        stream_in,
        segment_ids,
        master_q,
        moment_q,
        second_q,
        grad_q,
        master_kv,
        moment_kv,
        second_kv,
        grad_kv,
    ):
        fresh = sections_call(
            n_dp,
            n_tensor,
            stream_in,
            segment_ids,
            (master_q, moment_q, second_q, grad_q),
            (master_kv, moment_kv, second_kv, grad_kv),
        )
        *states, result = write_call(fresh)
        return (*states, result[None])

    weight_spec = P("pipe", "dp", "tensor")
    return jax.shard_map(
        on_device,
        mesh=mesh,
        in_specs=(P("dp", None), P("dp", None)) + (weight_spec,) * 8,
        out_specs=(weight_spec,) * 7,
        check_vma=False,
    )
```

```python
import functools

import jax
import jax.numpy as jnp
from jax import lax
from jax.experimental import pallas as pl
from jax.experimental.pallas import tpu as pltpu
from jax.sharding import PartitionSpec as P

HEAD_DIM = 128
MESH = pl.DeviceIdType.MESH

beta_one = 0.9
beta_two = 0.999
adam_eps = 1e-08
learn_rate = 0.003
decay_rate = 0.1
adam_step = 10.0
norm_eps = 1e-05


def adamw(master, moment, second, gradient):
    moment_new = beta_one * moment + (1.0 - beta_one) * gradient
    second_new = beta_two * second + (1.0 - beta_two) * gradient * gradient
    fix_one = 1.0 - beta_one**adam_step
    fix_two = 1.0 - beta_two**adam_step
    step_dir = moment_new / fix_one / (jnp.sqrt(second_new / fix_two) + adam_eps)
    master_new = master - learn_rate * (step_dir + decay_rate * master)
    return (master_new, moment_new, second_new)


def write_kernel(*refs):
    count = (len(refs) - 1) // 2
    sems = refs[-1]
    copies = [
        pltpu.make_async_copy(refs[i], refs[count + i], sems.at[i]) for i in range(count)
    ]
    for copy in copies:
        copy.start()
    for copy in copies:
        copy.wait()


def write_call(arrays):
    return pl.pallas_call(
        write_kernel,
        in_specs=[pl.BlockSpec(memory_space=pltpu.VMEM)] * len(arrays),
        out_specs=[pl.BlockSpec(memory_space=pl.ANY)] * len(arrays),
        out_shape=[jax.ShapeDtypeStruct(a.shape, a.dtype) for a in arrays],
        scratch_shapes=[pltpu.SemaphoreType.DMA((len(arrays),))],
    )(*[pltpu.with_memory_space_constraint(a, pltpu.VMEM) for a in arrays])


def sections_kernel(
    n_dp,
    n_tensor,
    x_hbm,
    seg_hbm,
    mq_hbm,
    eq_hbm,
    sq_hbm,
    gq_hbm,
    mk_hbm,
    ek_hbm,
    sk_hbm,
    gk_hbm,
    nmq,
    neq,
    nsq,
    nmk,
    nek,
    nsk,
    out_ref,
    x_ref,
    seg_ref,
    q_ref,
    k_ref,
    load_sem,
    gathered,
    normed_ref,
    cos_ref,
    sin_ref,
    mask_ref,
    kv_ref,
    queries_ref,
    sums_ref,
    first_ref,
    stream_ref,
    lent_ref,
    send_sem,
    recv_sem,
    pair_sem,
    stream_recv,
    lent_sem,
    go_sem,
):
    dp = lax.axis_index("dp")
    pipe = lax.axis_index("pipe")
    tensor = lax.axis_index("tensor")
    tokens, features = x_ref.shape
    rows = q_ref.shape[1]
    heads = first_ref.shape[0]
    n_pieces = 1 + heads
    half_rows = rows // 2
    relayed = n_dp == 4
    half = n_tensor // 2
    pair = lax.rem(tensor + half, n_tensor)
    holds_key = tensor < half
    slot = jnp.where(holds_key, 0, 1)
    f32 = jnp.float32
    bf16 = jnp.bfloat16

    if n_tensor == 4:
        far_first = [3 - tensor, pair, tensor + 1 - 2 * lax.rem(tensor, 2), tensor]
    else:
        far_first = [lax.rem(tensor + off, n_tensor) for off in range(n_tensor)]
    lent = (2, 3) if n_dp == 4 and heads == 3 else ()
    blockwise = rows == heads * HEAD_DIM and n_dp == n_tensor

    x_side = dp + 1 - 2 * lax.rem(dp, 2)
    y_side = lax.rem(dp + 2, n_dp)

    barrier = pltpu.get_barrier_semaphore()
    if relayed:
        near = [x_side, y_side, 3 - dp]
    else:
        near = [lax.rem(dp + off, n_dp) for off in range(1, n_dp)]
    for peer in near:
        pl.semaphore_signal(
            barrier, inc=1, device_id=(peer, pipe, tensor), device_id_type=MESH
        )
    pl.semaphore_signal(barrier, inc=1, device_id=(dp, pipe, pair), device_id_type=MESH)
    for t in far_first[1:] if n_tensor == 4 else far_first:
        pl.semaphore_signal(
            barrier, inc=1, device_id=(dp, 1 - pipe, t), device_id_type=MESH
        )

    load_x = pltpu.make_async_copy(x_hbm, x_ref, load_sem.at[2])
    load_seg = pltpu.make_async_copy(seg_hbm, seg_ref, load_sem.at[3])
    for n, ref in enumerate((mk_hbm, ek_hbm, sk_hbm, gk_hbm)):
        pltpu.make_async_copy(ref.at[0], k_ref.at[n], load_sem.at[0]).start()
    for n, ref in enumerate((mq_hbm, eq_hbm, sq_hbm, gq_hbm)):
        pltpu.make_async_copy(ref.at[0], q_ref.at[n], load_sem.at[1]).start()
    load_x.start()
    load_seg.start()

    def norm(read_block):
        blocks = features // HEAD_DIM
        squares = jnp.zeros((tokens, HEAD_DIM), f32)
        for b in range(blocks):
            value = read_block(b)
            squares += value * value
        mean = jnp.sum(squares, axis=1, keepdims=True) / features
        scale = lax.rsqrt(mean + norm_eps)
        for b in range(blocks):
            normed_ref[:, b * HEAD_DIM : (b + 1) * HEAD_DIM] = (
                read_block(b) * scale
            ).astype(bf16)

    def tables():
        row = lax.broadcasted_iota(jnp.int32, (tokens, tokens), 0)
        col = lax.broadcasted_iota(jnp.int32, (tokens, tokens), 1)
        seg_row = jnp.broadcast_to(seg_ref[...].astype(f32), (tokens, tokens))
        seg_col = jnp.sum(jnp.where(row == col, seg_row, 0.0), axis=1, keepdims=True)
        same = seg_row == seg_col
        mask_ref[...] = jnp.where(same & (col <= row), 1.0, 0.0)
        position = jnp.sum(jnp.where(same & (col < row), 1.0, 0.0), axis=1, keepdims=True)
        lane = lax.broadcasted_iota(jnp.int32, (1, HEAD_DIM), 1)
        half_dim = HEAD_DIM // 2
        index = jnp.where(lane < half_dim, lane, lane - half_dim).astype(f32)
        inverse_freq = 10000.0 ** (-2.0 * index / HEAD_DIM)
        angles = position * inverse_freq
        cos_ref[...] = jnp.cos(angles)
        sine = jnp.sin(angles)
        sin_ref[...] = jnp.where(lane < half_dim, -sine, sine)

    step_rows = 48 if rows % 48 == 0 else rows

    def update_k(i, carry):
        at = pl.ds(pl.multiple_of(i * step_rows, step_rows), step_rows)
        new = adamw(k_ref[0, at], k_ref[1, at], k_ref[2, at], k_ref[3, at])
        nmk[0, at], nek[0, at], nsk[0, at] = new
        gathered[0, dp, at] = new[0].astype(bf16)
        return carry

    def update_q(head):
        columns = slice(head * HEAD_DIM, (head + 1) * HEAD_DIM)

        def step(i, carry):
            at = pl.ds(pl.multiple_of(i * step_rows, step_rows), step_rows)
            new = adamw(*[q_ref[n, at, columns] for n in range(4)])
            nmq[0, at, columns], neq[0, at, columns], nsq[0, at, columns] = new
            gathered[1 + head, dp, at] = new[0].astype(bf16)
            return carry

        lax.fori_loop(0, rows // step_rows, step, 0)

    part_a = pl.ds(0, half_rows)
    part_b = pl.ds(half_rows, half_rows)

    def copy_to(peer, ref, piece, kind, group=0):
        return pltpu.make_async_remote_copy(
            src_ref=ref,
            dst_ref=ref,
            send_sem=send_sem.at[group],
            recv_sem=recv_sem.at[piece, kind],
            device_id=(peer, pipe, tensor),
            device_id_type=MESH,
        )

    def direct_copies(piece):
        own = gathered.at[piece, dp]
        peers = [3 - dp, x_side, y_side] if relayed else near
        return [copy_to(peer, own, piece, 2) for peer in peers]

    def own_copies(piece, kinds=range(4)):
        peers = (x_side, y_side, x_side, y_side)
        parts = (part_a, part_b, part_b, part_a)
        return [
            copy_to(peers[n], gathered.at[piece, dp, parts[n]], piece, min(n, 2))
            for n in kinds
        ]

    def relay_copies(piece):
        group = 2 if piece in lent else 0
        return [
            copy_to(y_side, gathered.at[piece, x_side, part_a], piece, 2, group),
            copy_to(x_side, gathered.at[piece, y_side, part_b], piece, 2, group),
        ]

    def send(piece, direct):
        for copy in direct_copies(piece) if direct or not relayed else own_copies(piece):
            copy.start()

    def relay(piece):
        if not relayed:
            return
        for got, passed in zip(own_copies(piece, (0, 1)), relay_copies(piece)):
            got.wait_recv()
            passed.start()

    def arrived(piece, direct):
        rest = n_dp - 1 if direct or not relayed else n_dp - 2
        copy_to(x_side, gathered.at[piece, pl.ds(0, rest)], piece, 2).wait_recv()

    def all_sent(blocks, group):
        copy_to(x_side, blocks, 0, 2, group).wait_send()

    def weights(piece):
        return gathered[piece].reshape(n_dp * rows, HEAD_DIM)

    def rope(values, cosine, sine):
        return values * cosine + pltpu.roll(values, HEAD_DIM // 2, 1) * sine

    def key_or_value(values, is_key):
        cosine = jnp.where(is_key, cos_ref[...], 1.0)
        sine = jnp.where(is_key, sin_ref[...], 0.0)
        return rope(values, cosine, sine).astype(bf16)

    def project(head):
        queries = jnp.dot(normed_ref[...], weights(1 + head), preferred_element_type=f32)
        queries_ref[head] = rope(queries, cos_ref[...], sin_ref[...]).astype(bf16)

    def mix(queries):
        scores = lax.dot_general(
            queries, kv_ref[0], (((1,), (1,)), ((), ())), preferred_element_type=f32
        ) * HEAD_DIM ** (-0.5)
        scores = scores.reshape(-1, tokens, tokens)
        scores = jnp.where(mask_ref[...][None] > 0.5, scores, -1e30)
        row_max = jnp.max(scores, axis=2, keepdims=True)
        terms = jnp.exp(scores - row_max)
        probs = (terms / jnp.sum(terms, axis=2, keepdims=True)).astype(bf16)
        return jnp.dot(
            probs.reshape(-1, tokens), kv_ref[1], preferred_element_type=f32
        )

    def attend(head, residual):
        return (residual.astype(f32) + mix(queries_ref[head])).astype(bf16)

    def pair_block(source, target):
        return pltpu.make_async_remote_copy(
            src_ref=source,
            dst_ref=target,
            send_sem=pair_sem.at[0],
            recv_sem=pair_sem.at[1],
            device_id=(dp, pipe, pair),
            device_id_type=MESH,
        )

    def stream_copy(head, to_tensor):
        return pltpu.make_async_remote_copy(
            src_ref=first_ref.at[head],
            dst_ref=stream_ref.at[tensor * heads + head],
            send_sem=send_sem.at[1],
            recv_sem=stream_recv.at[tensor],
            device_id=(dp, 1, to_tensor),
            device_id_type=MESH,
        )

    def stream_group(blocks, source):
        return pltpu.make_async_remote_copy(
            src_ref=blocks,
            dst_ref=blocks,
            send_sem=send_sem.at[1],
            recv_sem=stream_recv.at[source],
            device_id=(dp, 1 - pipe, tensor),
            device_id_type=MESH,
        )

    def lend(piece):
        return pltpu.make_async_remote_copy(
            src_ref=gathered.at[piece, dp],
            dst_ref=lent_ref.at[lent.index(piece)],
            send_sem=lent_sem.at[0],
            recv_sem=lent_sem.at[1],
            device_id=(dp, 0, tensor),
            device_id_type=MESH,
        )

    def lent_group():
        return pltpu.make_async_remote_copy(
            src_ref=lent_ref,
            dst_ref=lent_ref,
            send_sem=lent_sem.at[0],
            recv_sem=lent_sem.at[1],
            device_id=(dp, 1 - pipe, tensor),
            device_id_type=MESH,
        )

    def send_lent(piece):
        peers = (x_side, y_side, x_side, y_side)
        parts = (part_a, part_b, part_b, part_a)
        for n in range(4):
            pltpu.make_async_remote_copy(
                src_ref=lent_ref.at[lent.index(piece), parts[n]],
                dst_ref=gathered.at[piece, dp, parts[n]],
                send_sem=send_sem.at[2],
                recv_sem=recv_sem.at[piece, min(n, 2)],
                device_id=(peers[n], 1, tensor),
                device_id_type=MESH,
            ).start()

    weight_exchange = pair_block(gathered.at[0, dp], gathered.at[n_pieces, dp])

    pltpu.make_async_copy(k_ref, k_ref, load_sem.at[0]).wait()
    lax.fori_loop(0, rows // step_rows, update_k, 0)
    pl.semaphore_wait(barrier, len(near) + 1 + n_tensor - (n_tensor == 4))

    @pl.when(pipe == 0)
    def _():
        send(0, True)

    @pl.when(pipe == 1)
    def _():
        weight_exchange.start()

    pltpu.make_async_copy(q_ref, q_ref, load_sem.at[1]).wait()
    for head in range(heads):
        update_q(head)

        @pl.when(pipe == 0)
        def _():
            send(1 + head, True)

        if 1 + head in lent:

            @pl.when(pipe == 1)
            def _():
                lend(1 + head).start()

    load_x.wait()
    load_seg.wait()

    @pl.when(pipe == 0)
    def _():
        norm(lambda b: x_ref[:, b * HEAD_DIM : (b + 1) * HEAD_DIM].astype(f32))
        tables()
        exchange = pair_block(kv_ref.at[slot], kv_ref.at[slot])
        if lent:
            lent_group().wait_recv()
            for p in lent:
                send_lent(p)
        arrived(0, True)
        block = jnp.dot(normed_ref[...], weights(0), preferred_element_type=f32)
        kv_ref[slot] = key_or_value(block, holds_key)
        exchange.start()
        for head in range(heads):
            arrived(1 + head, True)
            if head == 0:
                pl.semaphore_signal(
                    go_sem, inc=1, device_id=(dp, 1, tensor), device_id_type=MESH
                )
            project(head)
            if head == 0:
                exchange.wait()
            columns = pl.ds(
                pl.multiple_of((tensor * heads + head) * HEAD_DIM, HEAD_DIM), HEAD_DIM
            )
            result = attend(head, x_ref[:, columns])
            first_ref[head] = result
            for t in far_first:
                stream_copy(head, t).start()
            out_ref[:, head * HEAD_DIM : (head + 1) * HEAD_DIM] = result
        all_sent(gathered.at[pl.ds(0, n_pieces), pl.ds(0, n_dp - 1)], 0)
        if lent:
            all_sent(gathered.at[0], 2)
        stream_group(stream_ref, 0).wait_send()

    @pl.when(pipe == 1)
    def _():
        tables()
        weight_exchange.wait()
        order = [0, n_pieces] + list(range(1, n_pieces))
        if lent:
            order = [0, n_pieces, 2, 3, 1]
        pl.semaphore_wait(go_sem, 1)
        for p in order:
            if p not in lent:
                send(p, False)
        for p in [0, 2, n_pieces, 3, 1] if lent else order:
            relay(p)
        early = order[:-2] if blockwise else order
        late = order[len(early) :]
        for p in early:
            arrived(p, False)

        def stream_arrived(source):
            blocks = stream_ref.at[pl.ds(source * heads, heads)]
            stream_group(blocks, source).wait_recv()

        if blockwise:
            sources = far_first[::-1]
            split = len(early) * HEAD_DIM

            def source_block(source):
                return jnp.concatenate(
                    [stream_ref[source * heads + h] for h in range(heads)], axis=1
                )

            def product(source, pieces):
                return jnp.dot(
                    source_block(source),
                    jnp.concatenate([gathered[p, source] for p in pieces], axis=1),
                    preferred_element_type=f32,
                )

            def add_squares(source, squares):
                for h in range(heads):
                    value = stream_ref[source * heads + h].astype(f32)
                    squares += value * value
                return squares

            squares = jnp.zeros((tokens, HEAD_DIM), f32)
            for n, source in enumerate(sources):
                stream_arrived(source)
                squares = add_squares(source, squares)
                block = product(source, early)
                if n == 0:
                    sums_ref[:, :split] = block
                else:
                    sums_ref[:, :split] += block
            mean = jnp.sum(squares, axis=1, keepdims=True) / features
            scale = lax.rsqrt(mean + norm_eps)

            def projected(n):
                return sums_ref[:, n * HEAD_DIM : (n + 1) * HEAD_DIM] * scale

        else:
            for source in far_first:
                stream_arrived(source)
            norm(lambda b: stream_ref[b].astype(f32))

            def projected(n):
                return jnp.dot(
                    normed_ref[...], weights(order[n]), preferred_element_type=f32
                )

        kv_ref[slot] = key_or_value(projected(0), holds_key)
        kv_ref[1 - slot] = key_or_value(projected(1), jnp.logical_not(holds_key))
        for p in late:
            arrived(p, False)
        if late:
            block = product(sources[0], late)
            for source in sources[1:]:
                block += product(source, late)
            sums_ref[:, split:] = block
        queries = [
            rope(projected(order.index(1 + head)), cos_ref[...], sin_ref[...]).astype(bf16)
            for head in range(heads)
        ]
        mixed = mix(jnp.concatenate(queries, axis=0))
        for head in range(heads):
            residual = stream_ref[tensor * heads + head].astype(f32)
            out_ref[:, head * HEAD_DIM : (head + 1) * HEAD_DIM] = (
                residual + mixed[head * tokens : (head + 1) * tokens]
            ).astype(bf16)
        rest = n_pieces + 1 - len(lent)
        all_sent(gathered.at[pl.ds(0, rest), pl.ds(0, n_dp - 1)], 0)
        if lent:
            all_sent(gathered.at[0, pl.ds(0, len(lent))], 2)
            lent_group().wait_send()


def sections_call(n_dp, n_tensor, stream, segments, q_arrays, kv_arrays):
    tokens, features = stream.shape
    _, rows, q_cols = q_arrays[0].shape
    kv_cols = kv_arrays[0].shape[2]
    heads = q_cols // HEAD_DIM
    n_pieces = 1 + heads
    bf16 = jnp.bfloat16
    f32 = jnp.float32
    vmem = pl.BlockSpec(memory_space=pltpu.VMEM)
    anywhere = pl.BlockSpec(memory_space=pl.ANY)
    return pl.pallas_call(
        functools.partial(sections_kernel, n_dp, n_tensor),
        out_shape=[pltpu.VMEM((1, rows, q_cols), f32)] * 3
        + [pltpu.VMEM((1, rows, kv_cols), f32)] * 3
        + [pltpu.VMEM((tokens, q_cols), bf16)],
        in_specs=[anywhere] * 10,
        out_specs=[vmem] * 7,
        scratch_shapes=[
            pltpu.VMEM((tokens, features), bf16),
            pltpu.VMEM(segments.shape, jnp.int32),
            pltpu.VMEM((4, rows, q_cols), f32),
            pltpu.VMEM((4, rows, kv_cols), f32),
            pltpu.SemaphoreType.DMA((4,)),
            pltpu.VMEM((n_pieces + 1, n_dp, rows, HEAD_DIM), bf16),
            pltpu.VMEM((tokens, features), bf16),
            pltpu.VMEM((tokens, HEAD_DIM), jnp.float32),
            pltpu.VMEM((tokens, HEAD_DIM), jnp.float32),
            pltpu.VMEM((tokens, tokens), jnp.float32),
            pltpu.VMEM((2, tokens, HEAD_DIM), bf16),
            pltpu.VMEM((heads, tokens, HEAD_DIM), bf16),
            pltpu.VMEM((tokens, (n_pieces + 1) * HEAD_DIM), f32),
            pltpu.VMEM((heads, tokens, HEAD_DIM), bf16),
            pltpu.VMEM((n_tensor * heads, tokens, HEAD_DIM), bf16),
            pltpu.VMEM((2, rows, HEAD_DIM), bf16),
            pltpu.SemaphoreType.DMA((3,)),
            pltpu.SemaphoreType.DMA((n_pieces + 1, 3)),
            pltpu.SemaphoreType.DMA((2,)),
            pltpu.SemaphoreType.DMA((n_tensor,)),
            pltpu.SemaphoreType.DMA((2,)),
            pltpu.SemaphoreType.REGULAR,
        ],
        compiler_params=pltpu.CompilerParams(collective_id=0, has_side_effects=True),
    )(stream, segments, *q_arrays, *kv_arrays)


def solution(mesh):
    n_dp, n_tensor = mesh.shape["dp"], mesh.shape["tensor"]

    def on_device(
        stream_in,
        segment_ids,
        master_q,
        moment_q,
        second_q,
        grad_q,
        master_kv,
        moment_kv,
        second_kv,
        grad_kv,
    ):
        fresh = sections_call(
            n_dp,
            n_tensor,
            stream_in,
            segment_ids,
            (master_q, moment_q, second_q, grad_q),
            (master_kv, moment_kv, second_kv, grad_kv),
        )
        *states, result = write_call(fresh)
        return (*states, result[None])

    weight_spec = P("pipe", "dp", "tensor")
    return jax.shard_map(
        on_device,
        mesh=mesh,
        in_specs=(P("dp", None), P("dp", None)) + (weight_spec,) * 8,
        out_specs=(weight_spec,) * 7,
        check_vma=False,
    )
```
